256 devices in a mesh: row: 32 (over y, x, core), head: 8 (over z).
Axes of the slice: x: 4, y: 4, z: 8, core: 2. Of those that a mesh axis runs over, the one named last changes fastest.
Arguments:
- inputs: bfloat16 [4, 2048, 5120], P(None, 'row', 'head'), may hold values from -6 to 6
- w_qkv: bfloat16 [5120, 8, 896], P(None, 'head'), may hold values from -0.078125 to 0.078125
- kv_pool: bfloat16 [256, 8, 128, 256], P('row', 'head'), may hold values from -56 to 56, as said below
- source_block: int32 [1024], P('row'), may hold values from 0 to 255, as said below
- slot_table: int32 [2048, 8], P('row'), may hold values from 0 to 31, as said below
- lengths: int32 [2048], P('row'), may hold values from 1 to 8
- finished: int32 [4, 2048], P(None, 'row'), may hold values 0 or 1
Outputs:
- attended: bfloat16 [4, 2048, 5120], P(None, 'row', 'head')
The draws below stay inside these ranges and needn't reach their ends.
Inputs may be any that keep to these rules, and one draw needn't show every extreme that they name: `kv_pool`: keys lie in -56 to 56, values in -6 to 6. `source_block`: A device's 32 entries are distinct block ids; at most 2 of them lie in the 8 blocks of any one index of row, and each device has exactly 2 from some index. `slot_table`: entries are slots of the branch's own row index; groups of four consecutive branches may share a leading run of entries.
All inputs are finite; a program needn't handle non-finite values. No bound on the sum of `finished` on one device may be relied on, other than what follows from the above.
Results may differ from the reference program's by a relative error of at most 0.012.
The reference program's roundings to bfloat16 on the way count: a program that leaves them out, or rounds other values in their place, can miss the bound.
Values may be sent and summed in bfloat16 or wider, within the bound.
A program may use at most 128 MiB of HBM per device.

```python
import jax
import jax.numpy as jnp
from jax import lax

D = 5120
QH = 40
KVH = 8
HD = 128
GRP = 5
BLK = 128
MAXB = 8
STEPS = 4
BR_DEV = 64
SLOTS_DEV = 32
POOL_DEV = 8
CAP = 2
BRANCHES = 2048
POOL_BLOCKS = 256


def draw_kv_pool(key, part):
    first, second = jax.random.split(key)
    shape = (POOL_BLOCKS, KVH, BLK, HD)
    keys_part = jnp.clip(jax.random.normal(first, shape, jnp.float32), -6.0, 6.0)
    values = jnp.clip(jax.random.normal(second, shape, jnp.float32), -6.0, 6.0)
    return jnp.concatenate([keys_part, values], axis=-1).astype(jnp.bfloat16)


def draw_source_block(key, part):
    devices = POOL_BLOCKS // POOL_DEV

    def single(sub):
        first, second, third = jax.random.split(sub, 3)
        token = jnp.arange(devices * CAP, dtype=jnp.int32)
        owner = token // CAP
        copies = token % CAP
        order = jax.random.permutation(first, devices * CAP).astype(jnp.int32)
        chosen = jax.random.randint(second, (), 0, devices)
        priority = jnp.where(owner == chosen, copies - CAP, order)
        ranked = jnp.argsort(priority, stable=True)[:SLOTS_DEV]
        offset = jax.random.randint(third, (devices,), 0, POOL_DEV)
        ident = owner * POOL_DEV + (offset[owner] + copies) % POOL_DEV
        return ident[ranked]
    subs = jax.random.split(key, devices)
    return jax.vmap(single)(subs).reshape(-1).astype(jnp.int32)


def draw_slot_table(key, part):
    first, second, third = jax.random.split(key, 3)
    trunk = jax.random.randint(first, (BRANCHES // 4, MAXB), 0, SLOTS_DEV)
    own = jax.random.randint(second, (BRANCHES, MAXB), 0, SLOTS_DEV)
    fork = jax.random.randint(third, (BRANCHES, 1), 0, MAXB + 1)
    shared = jnp.repeat(trunk, 4, axis=0)
    return jnp.where(jnp.arange(MAXB)[None, :] < fork, shared, own).astype(jnp.int32)


def plant(entries, stream_key, low, largest):
    shape = entries.shape
    spot = [jax.random.randint(jax.random.fold_in(stream_key, axis), (), 0, shape[axis]) for axis in range(len(shape))]
    entries = entries.at[tuple(spot)].set(low)
    longest = shape.index(max(shape))
    spot[longest] = (spot[longest] + 1) % shape[longest]
    return entries.at[tuple(spot)].set(largest)


def level_of(own_key, dims, shards, least, largest):
    def one(position, blocks):
        steps = jax.random.uniform(jax.random.fold_in(jax.random.fold_in(own_key, 6), position), (blocks,), jnp.float32, least / len(shards), largest / len(shards))
        return jnp.repeat(jnp.exp(steps), dims[position] // blocks).reshape((-1,) + (1,) * (len(dims) - position - 1))

    level = one(*shards[0])
    for cut in shards[1:]:
        level = level * one(*cut)
    return level


def normal_values(stream_key, extent, deviation, reach, shards=(), held_as=jnp.bfloat16):
    level = level_of(stream_key, extent, shards, -0.22, 0.18) if shards else 1.0
    entries = jax.random.normal(stream_key, extent, jnp.float32) * deviation * level
    return jnp.minimum(jnp.maximum(entries, -reach), reach).astype(held_as)


def setup_inputs(seed: int = 0) -> dict:
    arg_keys = jax.random.split(jax.random.key(seed), 8)
    inputs = normal_values(arg_keys[0], (STEPS, BRANCHES, D), 1.0, 6.0, ((1, 32), (2, 8)))
    w_qkv = normal_values(arg_keys[1], (D, KVH, (GRP + 2) * HD), D ** -0.5, 0.078125, ((1, 8),))
    kv_pool = draw_kv_pool(jax.random.fold_in(arg_keys[7], 71), 0)
    source_block = draw_source_block(jax.random.fold_in(arg_keys[7], 71), 0)
    slot_table = draw_slot_table(jax.random.fold_in(arg_keys[7], 71), 0)
    lengths = plant(jax.random.randint(arg_keys[5], (BRANCHES,), 1, MAXB + 1), jax.random.fold_in(arg_keys[5], 1), 1, MAXB).astype(jnp.int32)
    finished = plant((jax.random.randint(arg_keys[6], (STEPS, BRANCHES), 0, 4) < 1).astype(jnp.int32), jax.random.fold_in(arg_keys[6], 1), 0, 1)
    return {"inputs": inputs, "w_qkv": w_qkv, "kv_pool": kv_pool, "source_block": source_block, "slot_table": slot_table, "lengths": lengths, "finished": finished}


def membership(rows, counts):
    used = jnp.arange(MAXB)[None, :] < counts[:, None]
    hit = (rows[:, :, None] == jnp.arange(SLOTS_DEV)[None, None, :]) & used[:, :, None]
    return jnp.any(hit, axis=1)


def attend(query, new_keys, new_values, slots, member, done):
    keys = slots[..., :HD].astype(jnp.float32)
    values = slots[..., HD:].astype(jnp.float32)
    fresh_keys = new_keys.astype(jnp.float32)
    fresh_values = new_values.astype(jnp.float32)
    scale = HD ** -0.5
    order = jnp.arange(STEPS)
    outputs = []
    for step in range(STEPS):
        query_now = query[step].astype(jnp.float32)
        older = jnp.einsum("bhge,lhke->bhglk", query_now, keys) * scale
        older = jnp.where(member[:, None, None, :, None], older, -1.0e30)
        newer = jnp.einsum("bhge,ubhe->bhgu", query_now, fresh_keys) * scale
        newer = jnp.where(order <= step, newer, -1.0e30)
        top = jnp.maximum(jnp.max(older, axis=(3, 4)), jnp.max(newer, axis=3))
        exp_old = jnp.exp(older - top[..., None, None])
        exp_new = jnp.exp(newer - top[..., None])
        total = jnp.sum(exp_old, axis=(3, 4)) + jnp.sum(exp_new, axis=3)
        prob_old = (exp_old / total[..., None, None]).astype(jnp.bfloat16)
        prob_new = (exp_new / total[..., None]).astype(jnp.bfloat16)
        mixed = jnp.einsum("bhglk,lhke->bhge", prob_old.astype(jnp.float32), values)
        mixed = mixed + jnp.einsum("bhgu,ubhe->bhge", prob_new.astype(jnp.float32), fresh_values)
        mixed = mixed.astype(jnp.bfloat16)
        mixed = jnp.where(done[step][:, None, None, None] > 0, jnp.zeros_like(mixed), mixed)
        outputs.append(mixed.reshape(mixed.shape[0], -1))
    return jnp.stack(outputs)


def reference(inputs, w_qkv, kv_pool, source_block, slot_table, lengths, finished):
    devices = POOL_BLOCKS // POOL_DEV
    flat = jnp.dot(inputs.reshape(STEPS * BRANCHES, D), w_qkv.reshape(D, -1), preferred_element_type=jnp.float32)
    qkv = flat.astype(jnp.bfloat16).reshape(STEPS, devices, BR_DEV, KVH, GRP + 2, HD)
    qkv = jnp.moveaxis(qkv, 1, 0)
    query = qkv[..., :GRP, :]
    new_keys = qkv[..., GRP, :]
    new_values = qkv[..., GRP + 1, :]
    sources = source_block.reshape(devices, SLOTS_DEV)
    rows = slot_table.reshape(devices, BR_DEV, MAXB)
    counts = lengths.reshape(devices, BR_DEV)
    done = jnp.moveaxis(finished.reshape(STEPS, devices, BR_DEV), 1, 0)

    def device(items):
        q_d, k_d, v_d, s_d, r_d, c_d, f_d = items
        slots = kv_pool[s_d]
        return attend(q_d, k_d, v_d, slots, membership(r_d, c_d), f_d)

    result = lax.map(device, (query, new_keys, new_values, sources, rows, counts, done))
    return jnp.moveaxis(result, 0, 1).reshape(STEPS, BRANCHES, QH * HD)
```

```python
import jax
import jax.numpy as jnp
from jax import lax
from jax.experimental import pallas as pl
from jax.experimental.pallas import tpu as pltpu
from jax.sharding import PartitionSpec as P

HD = 128
GRP = 5
SIDE = 4
RING = 8
STEPS = 4
BR = 64
ROWS = STEPS * BR
SLOTS = 32
POOL = 8
PART = 640
WIDTH = RING * PART
COLS = (GRP + 2) * HD
OLD = SLOTS * HD
NEG = -1.0e30
SCALE = HD ** (-0.5) * 1.4426950408889634
OFFSETS = (0, 1, 3, 2)
MESH = pl.DeviceIdType.MESH
NT = (((1,), (1,)), ((), ()))


def device_row(y, x, core):
    return (y * SIDE + x) * 2 + core


def kernel(
    x_hbm, w_hbm, kv_hbm, sb, slots, lens, fin, out,
    xb, wb, acc, k0, k1, k2, k3, v0, v1, v2, v3, kpack, vpack, kpass, vpass, kr, vr, asks, asked,
    qa, ka, va, keep,
    load_sem, ask_send, ask_recv, z_send, z_recv, r_send, r_recv, p_send, p_recv, f_send, t_recv, s_recv,
):
    row = lax.axis_index("row")
    head = lax.axis_index("head")
    core = lax.rem(row, 2)
    x = lax.rem(lax.div(row, 2), SIDE)
    y = lax.div(row, 2 * SIDE)

    def around(position, offset, size):
        return lax.rem(position + offset, size)

    started = []

    def send(src, dst, send_sem, recv_sem, to_row, to_head):
        copy = pltpu.make_async_remote_copy(
            src_ref=src, dst_ref=dst, send_sem=send_sem, recv_sem=recv_sem,
            device_id=(to_row, to_head), device_id_type=MESH,
        )
        copy.start()
        started.append(copy)

    above = around(head, 1, RING)
    below = around(head, RING - 1, RING)

    def arrived(dst, recv_sem):
        pltpu.make_async_remote_copy(
            src_ref=dst, dst_ref=dst, send_sem=ask_send.at[0], recv_sem=recv_sem,
            device_id=(row, above), device_id_type=MESH,
        ).wait_recv()

    load_k = pltpu.make_async_copy(kv_hbm.at[:, :, pl.ds(0, HD)], k0, load_sem.at[0])
    load_v = pltpu.make_async_copy(kv_hbm.at[:, :, pl.ds(HD, HD)], v0, load_sem.at[1])
    load_x = pltpu.make_async_copy(x_hbm, xb.at[head], load_sem.at[2])
    load_w = pltpu.make_async_copy(w_hbm, wb, load_sem.at[3])
    load_k.start()
    load_v.start()
    load_x.start()
    load_w.start()

    peers = [(device_row(y, x, 1 - core), 1, 1)]
    for step in (1, 2, 3):
        for other in (0, 1):
            back = 4 - step
            peers.append((device_row(around(y, step, SIDE), x, other), 2 + (back - 1) * 2, 2 + (step - 1) * 2 + other))
            peers.append((device_row(y, around(x, step, SIDE), other), 8 + (back - 1) * 2, 8 + (step - 1) * 2 + other))

    barrier = pltpu.get_barrier_semaphore()
    for peer, _, _ in peers:
        pl.semaphore_signal(barrier, inc=1, device_id=(peer, head), device_id_type=MESH)
    for level in (above, below):
        pl.semaphore_signal(barrier, inc=1, device_id=(row, level), device_id_type=MESH)

    lane = lax.broadcasted_iota(jnp.int32, (1, 128), 1)
    lowest = jnp.full((1, 128), POOL - 1, jnp.int32)
    highest = jnp.zeros((1, 128), jnp.int32)
    for slot in range(SLOTS):
        block = sb[slot]
        here = lane == jnp.full((1, 128), lax.shift_right_logical(block, 3), jnp.int32)
        inner = jnp.full((1, 128), lax.bitwise_and(block, 7), jnp.int32)
        lowest = jnp.where(here, jnp.minimum(lowest, inner), lowest)
        highest = jnp.where(here, jnp.maximum(highest, inner), highest)
    asks[0] = lowest * 8 + highest

    pl.semaphore_wait(barrier, len(peers) + 2)

    for index, (peer, base, mine) in enumerate(peers):
        place = base if base == 1 else base + core
        send(asks.at[0], asks.at[place], ask_send.at[mine], ask_recv.at[place], peer, head)

    ring_k = (k0, k1, k2, k3)
    ring_v = (v0, v1, v2, v3)
    halves = (pl.ds(0, 4), pl.ds(4, 4))

    def along(kind, offset):
        if kind == 0:
            return device_row(y, around(x, offset, SIDE), core)
        return device_row(around(y, offset, SIDE), x, core)

    def ring_start(kind):
        ring = (ring_k, ring_v)[kind]
        for part in (0, 1):
            half = halves[part]
            send(ring[0].at[half], ring[2].at[half], r_send.at[kind, 0, part], r_recv.at[kind, 0, part], along(kind, 1), head)
            half = halves[1 - part]
            send(ring[0].at[half], ring[1].at[half], r_send.at[kind, 1, part], r_recv.at[kind, 1, part], along(kind, 3), head)

    def ring_forward(kind):
        ring = (ring_k, ring_v)[kind]
        arrived(ring[2].at[halves[0]], r_recv.at[kind, 0, 0])
        send(ring[2].at[halves[0]], ring[3].at[halves[0]], r_send.at[kind, 0, 2], r_recv.at[kind, 0, 2], along(kind, 1), head)
        arrived(ring[1].at[halves[1]], r_recv.at[kind, 1, 0])
        send(ring[1].at[halves[1]], ring[3].at[halves[1]], r_send.at[kind, 1, 2], r_recv.at[kind, 1, 2], along(kind, 3), head)

    def ring_rest(kind):
        ring = (ring_k, ring_v)[kind]
        arrived(ring[2].at[halves[1]], r_recv.at[kind, 0, 1])
        arrived(ring[1].at[halves[0]], r_recv.at[kind, 1, 1])

    def ring_last(kind):
        ring = (ring_k, ring_v)[kind]
        arrived(ring[3].at[halves[0]], r_recv.at[kind, 0, 2])
        arrived(ring[3].at[halves[1]], r_recv.at[kind, 1, 2])

    order = ((0, 1, 2, 3), (2, 3, 0, 1))
    level_to = (above, below)

    def z_chunk(way, hop):
        return around(head, RING - hop if way == 0 else hop, RING)

    def z_send_piece(way, hop, piece):
        chunk = around(head, 0 if hop == 1 else (RING - hop + 1 if way == 0 else hop - 1), RING)
        ref = xb.at[chunk, piece]
        send(ref, ref, z_send.at[way, hop - 1, piece], z_recv.at[way, hop - 1, piece], row, level_to[way])

    def z_arrive(way, hop, turn, forward):
        piece = order[way][turn]
        arrived(xb.at[z_chunk(way, hop), piece], z_recv.at[way, hop - 1, piece])
        if forward:
            z_send_piece(way, hop + 1, piece)

    targets = ((1, 0), (1, 1), (3, 0), (3, 1), (2, 0), (2, 1), (0, None))
    urgent = (4, 5, 0, 2, 1, 3, 6)

    def across(kind, offset, to_core):
        if kind == 0:
            return device_row(around(y, offset, SIDE), x, to_core)
        return device_row(y, around(x, offset, SIDE), to_core)

    def source(kind, turn, offset=0, from_core=None):
        from_core = core if from_core is None else from_core
        if kind == 0:
            return device_row(around(y, offset, SIDE), around(x, OFFSETS[turn], SIDE), from_core)
        return device_row(around(y, OFFSETS[turn], SIDE), around(x, offset, SIDE), from_core)

    packs, passes, kept = (kpack, vpack), (kpass, vpass), (kr, vr)

    def pick(kind, turn, wish, dst):
        chunk = ((k0, k1, k2, k3), (v0, v1, v2, v3))[kind][turn]
        code = asked[wish, 0, source(kind, turn)]
        dst[0] = chunk[lax.bitwise_and(lax.shift_right_logical(code, 3), 7)]
        dst[1] = chunk[lax.bitwise_and(code, 7)]

    def spread(kind, turn):
        pack, got = packs[kind], kept[kind]
        own = source(kind, turn)
        for target in urgent:
            offset, to_core = targets[target]
            if target == 6:
                wish = 1
            else:
                wish = (2, 8)[kind] + (offset - 1) * 2 + to_core
            pick(kind, turn, wish, pack.at[target, turn])
        pick(kind, turn, 0, got.at[own])
        send(pack.at[4, turn], passes[kind].at[0, turn], p_send.at[kind, 4, turn], t_recv.at[kind, 0, turn], across(kind, 1, core), head)
        send(pack.at[5, turn], passes[kind].at[1, turn], p_send.at[kind, 5, turn], t_recv.at[kind, 1, turn], across(kind, 3, core), head)
        for target in (0, 2, 1, 3):
            offset, to_core = targets[target]
            seen = 1 if offset == 1 else 0
            send(pack.at[target, turn], got.at[own], p_send.at[kind, target, turn], p_recv.at[kind, seen, core, turn], across(kind, offset, to_core), head)
        send(pack.at[6, turn], got.at[own], p_send.at[kind, 6, turn], s_recv.at[kind, turn], device_row(y, x, 1 - core), head)

    def relay(kind, turn):
        got = kept[kind]
        for way in (0, 1):
            ref = passes[kind].at[way, turn]
            arrived(ref, t_recv.at[kind, way, turn])
            origin = source(kind, turn, 3 if way == 0 else 1)
            send(ref, got.at[origin], f_send.at[kind, way, turn], p_recv.at[kind, 2, core, turn], across(kind, 1 if way == 0 else 3, way), head)

    def project(chunk, first):
        part = jnp.dot(
            xb[chunk].reshape(ROWS, PART),
            wb[pl.ds(pl.multiple_of(chunk * PART, PART), PART), :],
            preferred_element_type=jnp.float32,
        )
        if first:
            acc[...] = part
        else:
            acc[...] += part

    load_k.wait()
    ring_start(0)
    load_v.wait()
    ring_start(1)
    load_x.wait()
    for turn in range(4):
        for way in (0, 1):
            z_send_piece(way, 1, order[way][turn])

    for _, _, mine in peers:
        arrived(asks.at[mine], ask_recv.at[mine])
    to_scalar = pltpu.make_async_copy(asks, asked, load_sem.at[4])
    to_scalar.start()
    to_scalar.wait()

    spread(0, 0)
    spread(1, 0)
    ring_forward(0)
    ring_forward(1)
    load_w.wait()
    project(head, True)
    for turn in (0, 1):
        for way in (0, 1):
            z_arrive(way, 1, turn, True)
    ring_rest(0)
    ring_rest(1)
    spread(0, 1)
    spread(1, 1)
    for turn in (2, 3):
        for way in (0, 1):
            z_arrive(way, 1, turn, True)
    spread(0, 2)
    spread(1, 2)
    relay(0, 0)
    relay(1, 0)
    project(z_chunk(0, 1), False)
    project(z_chunk(1, 1), False)
    for turn in (0, 1):
        for way in (0, 1):
            z_arrive(way, 2, turn, True)
    ring_last(0)
    ring_last(1)
    spread(0, 3)
    spread(1, 3)
    for turn in (2, 3):
        for way in (0, 1):
            z_arrive(way, 2, turn, True)
    relay(0, 1)
    relay(1, 1)
    project(z_chunk(0, 2), False)
    project(z_chunk(1, 2), False)
    for turn in (0, 1):
        for way in (0, 1):
            z_arrive(way, 3, turn, True)
    relay(0, 2)
    relay(1, 2)
    for turn in (2, 3):
        for way in (0, 1):
            z_arrive(way, 3, turn, False)
    relay(0, 3)
    relay(1, 3)
    project(z_chunk(0, 3), False)
    project(z_chunk(1, 3), False)
    for turn in (0, 1):
        for way in (0, 1):
            z_arrive(way, 4, turn, False)
    project(z_chunk(0, 4), False)

    eye = jnp.where(
        lax.broadcasted_iota(jnp.int32, (BR, BR), 0) == lax.broadcasted_iota(jnp.int32, (BR, BR), 1), 1.0, 0.0
    ).astype(jnp.bfloat16)
    slot_id = lax.broadcasted_iota(jnp.int32, (HD, BR), 0)
    outside = jnp.ones((HD, BR), jnp.float32)
    for entry in range(8):
        named = jnp.where(lens[...] > entry, slots[pl.ds(entry, 1), :], -1)
        outside = jnp.where(slot_id == jnp.broadcast_to(named, (HD, BR)), 0.0, outside)
    outside = lax.dot_general(eye, outside.astype(jnp.bfloat16), NT, preferred_element_type=jnp.float32).astype(jnp.bfloat16)
    for step in range(STEPS):
        going = jnp.where(fin[pl.ds(step, 1), :] > 0, 0.0, 1.0)
        going = jnp.broadcast_to(going, (HD, BR)).astype(jnp.bfloat16)
        keep[pl.ds(step * BR, BR), :] = lax.dot_general(eye, going, NT, preferred_element_type=jnp.float32)
        for group in range(GRP):
            qa[pl.ds(group * ROWS + step * BR, BR), pl.ds(HD, HD)] = outside
    for group in range(GRP):
        qa[pl.ds(group * ROWS, ROWS), pl.ds(0, HD)] = acc[:, pl.ds(group * HD, HD)].astype(jnp.bfloat16)
    column = lax.broadcasted_iota(jnp.int32, (HD, HD), 1)
    for slot in range(SLOTS):
        ka[pl.ds(slot * HD, HD), pl.ds(HD, HD)] = jnp.where(column == slot, NEG, 0.0).astype(jnp.bfloat16)
    ka[pl.ds(OLD, ROWS), pl.ds(0, HD)] = acc[:, pl.ds(GRP * HD, HD)].astype(jnp.bfloat16)
    ka[pl.ds(OLD, ROWS), pl.ds(HD, HD)] = jnp.zeros((ROWS, HD), jnp.bfloat16)
    va[pl.ds(OLD, ROWS), pl.ds(0, HD)] = acc[:, pl.ds((GRP + 1) * HD, HD)].astype(jnp.bfloat16)
    va[:, pl.ds(HD, HD)] = jnp.ones((OLD + ROWS, HD), jnp.bfloat16)

    for turn in range(4):
        for kind in (0, 1):
            got = kept[kind]
            for seen, offset in ((0, 1), (1, 3), (2, 2)):
                for from_core in (0, 1):
                    arrived(got.at[source(kind, turn, offset, from_core)], p_recv.at[kind, seen, from_core, turn])
            arrived(got.at[source(kind, turn, 0, 1 - core)], s_recv.at[kind, turn])
    for slot in range(SLOTS):
        block = sb[slot]
        device = lax.shift_right_logical(block, 3)
        code = asked[0, 0, device]
        second = jnp.where(lax.bitwise_and(block, 7) == lax.shift_right_logical(code, 3), 0, 1)
        ka[pl.ds(slot * HD, HD), pl.ds(0, HD)] = kr[device, second]
        va[pl.ds(slot * HD, HD), pl.ds(0, HD)] = vr[device, second]

    r = lax.broadcasted_iota(jnp.int32, (ROWS, ROWS), 0)
    q = lax.broadcasted_iota(jnp.int32, (ROWS, ROWS), 1)
    seen_new = jnp.logical_and(lax.bitwise_and(r, BR - 1) == lax.bitwise_and(q, BR - 1), q <= r)
    for group in range(GRP):
        query = qa[pl.ds(group * ROWS, ROWS), :]
        older = lax.dot_general(query, ka[pl.ds(0, OLD), :], NT, preferred_element_type=jnp.float32)
        newer = lax.dot_general(query, ka[pl.ds(OLD, ROWS), :], NT, preferred_element_type=jnp.float32)
        newer = jnp.where(seen_new, newer, NEG)
        top = jnp.maximum(jnp.max(older, axis=1, keepdims=True), jnp.max(newer, axis=1, keepdims=True))
        p_old = jnp.exp2((older - top) * SCALE).astype(jnp.bfloat16)
        p_new = jnp.exp2((newer - top) * SCALE).astype(jnp.bfloat16)
        mixed = jnp.dot(p_old, va[pl.ds(0, OLD), :], preferred_element_type=jnp.float32)
        mixed = mixed + jnp.dot(p_new, va[pl.ds(OLD, ROWS), :], preferred_element_type=jnp.float32)
        result = jnp.where(keep[...] > 0.5, mixed[:, :HD] / mixed[:, HD:], 0.0).astype(jnp.bfloat16)
        out[:, :, pl.ds(group * HD, HD)] = result.reshape(STEPS, BR, HD)

    for copy in started:
        copy.wait_send()


def shards(inputs, w_qkv, kv_pool, source_block, slot_table, lengths, finished):
    bf16 = jnp.bfloat16
    block = (HD, HD)
    any_space = pl.BlockSpec(memory_space=pl.ANY)
    vmem = pl.BlockSpec(memory_space=pltpu.VMEM)
    dma = pltpu.SemaphoreType.DMA
    return pl.pallas_call(
        kernel,
        out_shape=jax.ShapeDtypeStruct((STEPS, BR, GRP * HD), bf16),
        in_specs=[any_space, any_space, any_space, pl.BlockSpec(memory_space=pltpu.SMEM), vmem, vmem, vmem],
        out_specs=vmem,
        scratch_shapes=[
            pltpu.VMEM((RING, STEPS, BR, PART), bf16),
            pltpu.VMEM((WIDTH, COLS), bf16),
            pltpu.VMEM((ROWS, COLS), jnp.float32),
            *[pltpu.VMEM((POOL, *block), bf16) for _ in range(8)],
            pltpu.VMEM((7, 4, 2, *block), bf16),
            pltpu.VMEM((7, 4, 2, *block), bf16),
            pltpu.VMEM((2, 4, 2, *block), bf16),
            pltpu.VMEM((2, 4, 2, *block), bf16),
            pltpu.VMEM((SLOTS, 2, *block), bf16),
            pltpu.VMEM((SLOTS, 2, *block), bf16),
            pltpu.VMEM((14, 1, 128), jnp.int32),
            pltpu.SMEM((14, 1, 128), jnp.int32),
            pltpu.VMEM((GRP * ROWS, 2 * HD), bf16),
            pltpu.VMEM((OLD + ROWS, 2 * HD), bf16),
            pltpu.VMEM((OLD + ROWS, 2 * HD), bf16),
            pltpu.VMEM((ROWS, HD), jnp.float32),
            dma((5,)),
            dma((14,)),
            dma((14,)),
            dma((2, 4, 4)),
            dma((2, 4, 4)),
            dma((2, 2, 3)),
            dma((2, 2, 3)),
            dma((2, 7, 4)),
            dma((2, 3, 2, 4)),
            dma((2, 2, 4)),
            dma((2, 2, 4)),
            dma((2, 4)),
        ],
        compiler_params=pltpu.CompilerParams(
            collective_id=0, has_side_effects=True, vmem_limit_bytes=60 * 1024 * 1024
        ),
        name="rollout_attention",
    )(
        inputs,
        w_qkv.reshape(WIDTH, COLS),
        kv_pool.reshape(POOL, HD, 2 * HD),
        source_block,
        slot_table.T,
        lengths.reshape(1, BR),
        finished,
    )


def solution(mesh):
    placed = (
        P(None, "row", "head"),
        P(None, "head", None),
        P("row", "head", None, None),
        P("row"),
        P("row", None),
        P("row"),
        P(None, "row"),
    )
    return jax.shard_map(
        shards, mesh=mesh, in_specs=placed, out_specs=P(None, "row", "head"), check_vma=False
    )
```

```python
import jax
import jax.numpy as jnp
from jax import lax
from jax.experimental import pallas as pl
from jax.experimental.pallas import tpu as pltpu
from jax.sharding import PartitionSpec as P

HD = 128
GRP = 5
SIDE = 4
RING = 8
STEPS = 4
BR = 64
ROWS = STEPS * BR
SLOTS = 32
POOL = 8
PART = 640
WIDTH = RING * PART
COLS = (GRP + 2) * HD
OLD = SLOTS * HD
HALF = HD // 2
TALL = GRP * BR
NEG = -1.0e30
SCALE = HD ** (-0.5) * 1.4426950408889634
OFFSETS = (0, 1, 3, 2)
MESH = pl.DeviceIdType.MESH
NT = (((1,), (1,)), ((), ()))


def device_row(y, x, core):
    return (y * SIDE + x) * 2 + core


def kernel(
    x_hbm, w_hbm, kv_hbm, sb_hbm, slots_hbm, lens_hbm, fin_hbm, out,
    xb, wb, acc, *rest,
):
    rings = (rest[0:4], rest[4:8], rest[8:12], rest[12:16])
    packs = rest[16:20]
    kept = rest[20:24]
    (
        asks, asked, sb, slots, lens, fin, qa, ka, va, keep, prob,
        load_sem, ask_send, ask_recv, z_send, z_recv, r_send, r_recv, p_send, p_recv,
    ) = rest[24:]
    row = lax.axis_index("row")
    head = lax.axis_index("head")
    core = lax.rem(row, 2)
    x = lax.rem(lax.div(row, 2), SIDE)
    y = lax.div(row, 2 * SIDE)

    def around(position, offset, size):
        return lax.rem(position + offset, size)

    above = around(head, 1, RING)
    below = around(head, RING - 1, RING)

    peers = [(device_row(y, x, 1 - core), 1, 1)]
    for step in (1, 2, 3):
        for other in (0, 1):
            back = 4 - step
            peers.append((device_row(around(y, step, SIDE), x, other), 2 + (back - 1) * 2, 2 + (step - 1) * 2 + other))
            peers.append((device_row(y, around(x, step, SIDE), other), 8 + (back - 1) * 2, 8 + (step - 1) * 2 + other))

    barrier = pltpu.get_barrier_semaphore()
    for level in (above, below):
        pl.semaphore_signal(barrier, inc=1, device_id=(row, level), device_id_type=MESH)
    for peer, _, _ in peers:
        pl.semaphore_signal(barrier, inc=1, device_id=(peer, head), device_id_type=MESH)

    started = []

    def send(src, dst, send_sem, recv_sem, to_row, to_head):
        copy = pltpu.make_async_remote_copy(
            src_ref=src, dst_ref=dst, send_sem=send_sem, recv_sem=recv_sem,
            device_id=(to_row, to_head), device_id_type=MESH,
        )
        copy.start()
        started.append(copy)

    def arrived(dst, recv_sem):
        pltpu.make_async_remote_copy(
            src_ref=dst, dst_ref=dst, send_sem=ask_send.at[0], recv_sem=recv_sem,
            device_id=(row, above), device_id_type=MESH,
        ).wait_recv()

    def load(src, dst, index):
        copy = pltpu.make_async_copy(src, dst, load_sem.at[index])
        copy.start()
        return copy

    load_sb = load(sb_hbm, sb, 0)
    load_kv = [
        load(kv_hbm.at[:, pl.ds((kind % 2) * HALF, HALF), pl.ds((kind // 2) * HD, HD)], rings[kind][0], 1 + kind)
        for kind in range(4)
    ]
    load_x = load(x_hbm, xb.at[head], 5)
    load_small = [load(slots_hbm, slots, 6), load(lens_hbm, lens, 7), load(fin_hbm, fin, 8)]
    load_w = load(w_hbm, wb, 9)

    load_sb.wait()
    lane = lax.broadcasted_iota(jnp.int32, (1, 128), 1)
    lowest = jnp.full((1, 128), POOL - 1, jnp.int32)
    highest = jnp.zeros((1, 128), jnp.int32)
    for slot in range(SLOTS):
        block = sb[slot]
        here = lane == jnp.full((1, 128), lax.shift_right_logical(block, 3), jnp.int32)
        inner = jnp.full((1, 128), lax.bitwise_and(block, 7), jnp.int32)
        lowest = jnp.where(here, jnp.minimum(lowest, inner), lowest)
        highest = jnp.where(here, jnp.maximum(highest, inner), highest)
    asks[0] = lowest * 8 + highest
    for copy in load_kv:
        copy.wait()
    load_x.wait()

    pl.semaphore_wait(barrier, len(peers) + 2)

    quarters = (pl.ds(0, 4), pl.ds(4, 4))

    def along(kind, offset):
        if kind % 2 == 0:
            return device_row(y, around(x, offset, SIDE), core)
        return device_row(around(y, offset, SIDE), x, core)

    def ring_start(kind):
        ring = rings[kind]
        for part in (0, 1):
            half = quarters[part]
            send(ring[0].at[half], ring[2].at[half], r_send.at[kind, 0, part], r_recv.at[kind, 0, part], along(kind, 1), head)
            half = quarters[1 - part]
            send(ring[0].at[half], ring[1].at[half], r_send.at[kind, 1, part], r_recv.at[kind, 1, part], along(kind, 3), head)

    def ring_forward(kind):
        ring = rings[kind]
        arrived(ring[2].at[quarters[0]], r_recv.at[kind, 0, 0])
        send(ring[2].at[quarters[0]], ring[3].at[quarters[0]], r_send.at[kind, 0, 2], r_recv.at[kind, 0, 2], along(kind, 1), head)
        arrived(ring[1].at[quarters[1]], r_recv.at[kind, 1, 0])
        send(ring[1].at[quarters[1]], ring[3].at[quarters[1]], r_send.at[kind, 1, 2], r_recv.at[kind, 1, 2], along(kind, 3), head)

    def ring_rest(kind):
        arrived(rings[kind][2].at[quarters[1]], r_recv.at[kind, 0, 1])
        arrived(rings[kind][1].at[quarters[0]], r_recv.at[kind, 1, 1])

    def ring_last(kind):
        arrived(rings[kind][3].at[quarters[0]], r_recv.at[kind, 0, 2])
        arrived(rings[kind][3].at[quarters[1]], r_recv.at[kind, 1, 2])

    level_to = (above, below)

    def z_chunk(way, hop):
        return around(head, RING - hop if way == 0 else hop, RING)

    def z_piece(chunk, way, hop, step):
        if hop == 4:
            return xb.at[chunk, step, pl.ds(way * (BR // 2), BR // 2)]
        return xb.at[chunk, step]

    def z_out(hop, step):
        for way in (0, 1):
            chunk = head if hop == 1 else z_chunk(way, hop - 1)
            ref = z_piece(chunk, way, hop, step)
            send(ref, ref, z_send.at[way, hop - 1, step], z_recv.at[way, hop - 1, step], row, level_to[way])

    def z_in(hop, step, forward=True):
        for way in (0, 1):
            arrived(z_piece(z_chunk(way, hop), way, hop, step), z_recv.at[way, hop - 1, step])
        if forward:
            z_out(hop + 1, step)

    targets = ((2, 0), (2, 1), (1, 0), (3, 0), (1, 1), (3, 1), (0, None))
    batches = ((0, 1), (1, 2), (3, 1))

    def across(kind, offset, to_core):
        if kind % 2 == 0:
            return device_row(around(y, offset, SIDE), x, to_core)
        return device_row(y, around(x, offset, SIDE), to_core)

    def source(kind, turn):
        if kind % 2 == 0:
            return device_row(y, around(x, OFFSETS[turn], SIDE), core)
        return device_row(around(y, OFFSETS[turn], SIDE), x, core)

    def pick(kind, turn, wish, dst):
        chunk = rings[kind][turn]
        code = asked[wish, 0, source(kind, turn)]
        dst[0] = chunk[lax.bitwise_and(lax.shift_right_logical(code, 3), 7)]
        dst[1] = chunk[lax.bitwise_and(code, 7)]

    def spread(kind, batch):
        pack, got = packs[kind], kept[kind]
        first, count = batches[batch]
        for turn in range(first, first + count):
            for target, (offset, to_core) in enumerate(targets):
                wish = 1 if target == 6 else (2, 8)[kind % 2] + (offset - 1) * 2 + to_core
                pick(kind, turn, wish, pack.at[target, turn])
            pick(kind, turn, 0, got.at[0, core, turn])
        turns = pl.ds(first, count)
        for target, (offset, to_core) in enumerate(targets):
            seen = (4 - offset) % 4
            to_row = device_row(y, x, 1 - core) if target == 6 else across(kind, offset, to_core)
            send(pack.at[target, turns], got.at[seen, core, turns], p_send.at[kind, target, batch], p_recv.at[kind, seen, core, batch], to_row, head)

    def collect(kind):
        got = kept[kind]
        for batch in range(3):
            first, count = batches[batch]
            turns = pl.ds(first, count)
            for seen in (1, 3, 2):
                for from_core in (0, 1):
                    arrived(got.at[seen, from_core, turns], p_recv.at[kind, seen, from_core, batch])
            arrived(got.at[0, 1 - core, turns], p_recv.at[kind, 0, 1 - core, batch])

    def fill(table, kinds):
        for slot in range(SLOTS):
            block = sb[slot]
            device = lax.shift_right_logical(block, 3)
            code = asked[0, 0, device]
            second = jnp.where(lax.bitwise_and(block, 7) == lax.shift_right_logical(code, 3), 0, 1)
            from_core = lax.bitwise_and(device, 1)
            off_x = lax.bitwise_and(lax.shift_right_logical(device, 1) + SIDE - x, 3)
            off_y = lax.bitwise_and(lax.shift_right_logical(device, 3) + SIDE - y, 3)
            turn_x = lax.bitwise_xor(off_x, lax.shift_right_logical(off_x, 1))
            turn_y = lax.bitwise_xor(off_y, lax.shift_right_logical(off_y, 1))
            table[pl.ds(slot * HD, HALF), pl.ds(0, HD)] = kept[kinds[0]][off_y, from_core, turn_x, second]
            table[pl.ds(slot * HD + HALF, HALF), pl.ds(0, HD)] = kept[kinds[1]][off_x, from_core, turn_y, second]

    def project(chunk, pair, first=False):
        rows = pl.ds(pair * 2 * BR, 2 * BR)
        part = jnp.dot(
            xb[chunk, pl.ds(pair * 2, 2)].reshape(2 * BR, PART),
            wb[pl.ds(pl.multiple_of(chunk * PART, PART), PART), :],
            preferred_element_type=jnp.float32,
        )
        if first:
            acc[rows, :] = part
        else:
            acc[rows, :] += part

    def round_qkv(pair):
        bf16 = jnp.bfloat16
        for step in (2 * pair, 2 * pair + 1):
            rows = pl.ds(step * BR, BR)
            for group in range(GRP):
                qa[pl.ds(step * TALL + group * BR, BR), pl.ds(0, HD)] = acc[rows, pl.ds(group * HD, HD)].astype(bf16)
            ka[pl.ds(OLD + step * BR, BR), pl.ds(0, HD)] = acc[rows, pl.ds(GRP * HD, HD)].astype(bf16)
            va[pl.ds(OLD + step * BR, BR), pl.ds(0, HD)] = acc[rows, pl.ds((GRP + 1) * HD, HD)].astype(bf16)

    def softmax(step):
        query = qa[pl.ds(step * TALL, TALL), :]
        older = lax.dot_general(query, ka[pl.ds(0, OLD), :], NT, preferred_element_type=jnp.float32)
        newer = lax.dot_general(query, ka[pl.ds(OLD, ROWS), :], NT, preferred_element_type=jnp.float32)
        r = lax.broadcasted_iota(jnp.int32, (TALL, ROWS), 0)
        q = lax.broadcasted_iota(jnp.int32, (TALL, ROWS), 1)
        fresh = jnp.logical_and(lax.bitwise_and(r, BR - 1) == lax.bitwise_and(q, BR - 1), q < (step + 1) * BR)
        newer = jnp.where(fresh, newer, NEG)
        top = jnp.maximum(jnp.max(older, axis=1, keepdims=True), jnp.max(newer, axis=1, keepdims=True))
        prob[pl.ds(step * TALL, TALL), pl.ds(0, OLD)] = jnp.exp2((older - top) * SCALE).astype(jnp.bfloat16)
        prob[pl.ds(step * TALL, TALL), pl.ds(OLD, ROWS)] = jnp.exp2((newer - top) * SCALE).astype(jnp.bfloat16)

    def prepare():
        for copy in load_small:
            copy.wait()
        eye = jnp.where(
            lax.broadcasted_iota(jnp.int32, (BR, BR), 0) == lax.broadcasted_iota(jnp.int32, (BR, BR), 1), 1.0, 0.0
        ).astype(jnp.bfloat16)
        slot_id = lax.broadcasted_iota(jnp.int32, (HD, BR), 0)
        outside = jnp.ones((HD, BR), jnp.float32)
        for entry in range(8):
            named = jnp.where(lens[...] > entry, slots[pl.ds(entry, 1), :], -1)
            outside = jnp.where(slot_id == jnp.broadcast_to(named, (HD, BR)), 0.0, outside)
        outside = lax.dot_general(eye, outside.astype(jnp.bfloat16), NT, preferred_element_type=jnp.float32).astype(jnp.bfloat16)
        for step in range(STEPS):
            going = jnp.where(fin[pl.ds(step, 1), :] > 0, 0.0, 1.0)
            going = jnp.broadcast_to(going, (HD, BR)).astype(jnp.bfloat16)
            keep[pl.ds(step * BR, BR), :] = lax.dot_general(eye, going, NT, preferred_element_type=jnp.float32)
            for group in range(GRP):
                qa[pl.ds(step * TALL + group * BR, BR), pl.ds(HD, HD)] = outside
        column = lax.broadcasted_iota(jnp.int32, (HD, HD), 1)
        for slot in range(SLOTS):
            ka[pl.ds(slot * HD, HD), pl.ds(HD, HD)] = jnp.where(column == slot, NEG, 0.0).astype(jnp.bfloat16)
        ka[pl.ds(OLD, ROWS), :] = jnp.zeros((ROWS, 2 * HD), jnp.bfloat16)
        va[:, pl.ds(HD, HD)] = jnp.ones((OLD + ROWS, HD), jnp.bfloat16)

    for index, (peer, base, mine) in enumerate(peers):
        place = base if base == 1 else base + core
        send(asks.at[0], asks.at[place], ask_send.at[mine], ask_recv.at[place], peer, head)
    ring_start(0)
    ring_start(1)
    z_out(1, 0)
    z_out(1, 1)
    z_out(1, 2)
    ring_start(2)
    ring_start(3)
    prepare()
    ring_forward(0)
    ring_forward(1)
    z_in(1, 0)
    for _, _, mine in peers:
        arrived(asks.at[mine], ask_recv.at[mine])
    to_scalar = pltpu.make_async_copy(asks, asked, load_sem.at[10])
    to_scalar.start()
    to_scalar.wait()
    spread(0, 0)
    spread(1, 0)
    z_in(1, 1)
    ring_rest(0)
    ring_rest(1)
    spread(0, 1)
    spread(1, 1)
    load_w.wait()
    project(head, 0, True)
    project(head, 1, True)
    z_in(2, 0)
    ring_last(0)
    ring_last(1)
    spread(0, 2)
    spread(1, 2)
    z_in(2, 1)
    z_out(1, 3)
    ring_forward(2)
    ring_forward(3)
    project(z_chunk(0, 1), 0)
    project(z_chunk(1, 1), 0)
    spread(2, 0)
    spread(3, 0)
    z_in(3, 0)
    project(z_chunk(0, 2), 0)
    project(z_chunk(1, 2), 0)
    ring_rest(2)
    ring_rest(3)
    z_in(3, 1)
    z_in(1, 2)
    spread(2, 1)
    spread(3, 1)
    project(z_chunk(0, 3), 0)
    project(z_chunk(1, 3), 0)
    z_in(4, 0, False)
    z_in(1, 3)
    z_in(4, 1, False)
    project(z_chunk(0, 4), 0)
    round_qkv(0)
    ring_last(2)
    ring_last(3)
    spread(2, 2)
    spread(3, 2)
    collect(0)
    collect(1)
    fill(ka, (0, 1))
    z_in(2, 2)
    softmax(0)
    z_in(2, 3)
    project(z_chunk(0, 1), 1)
    project(z_chunk(1, 1), 1)
    z_in(3, 2)
    softmax(1)
    z_in(3, 3)
    project(z_chunk(0, 2), 1)
    project(z_chunk(1, 2), 1)
    project(z_chunk(0, 3), 1)
    project(z_chunk(1, 3), 1)
    z_in(4, 2, False)
    z_in(4, 3, False)
    project(z_chunk(0, 4), 1)
    round_qkv(1)
    softmax(2)
    softmax(3)
    collect(2)
    collect(3)
    fill(va, (2, 3))
    mixed = jnp.dot(prob[...], va[...], preferred_element_type=jnp.float32)
    for step in range(STEPS):
        going = keep[pl.ds(step * BR, BR), :] > 0.5
        for group in range(GRP):
            at = step * TALL + group * BR
            part = mixed[at : at + BR]
            result = jnp.where(going, part[:, :HD] / part[:, HD:], 0.0).astype(jnp.bfloat16)
            out[step, :, pl.ds(group * HD, HD)] = result

    for copy in started:
        copy.wait_send()


def shards(inputs, w_qkv, kv_pool, source_block, slot_table, lengths, finished):
    bf16 = jnp.bfloat16
    half = (HALF, HD)
    any_space = pl.BlockSpec(memory_space=pl.ANY)
    vmem = pl.BlockSpec(memory_space=pltpu.VMEM)
    dma = pltpu.SemaphoreType.DMA
    return pl.pallas_call(
        kernel,
        out_shape=jax.ShapeDtypeStruct((STEPS, BR, GRP * HD), bf16),
        in_specs=[any_space] * 7,
        out_specs=vmem,
        scratch_shapes=[
            pltpu.VMEM((RING, STEPS, BR, PART), bf16),
            pltpu.VMEM((WIDTH, COLS), bf16),
            pltpu.VMEM((ROWS, COLS), jnp.float32),
            *[pltpu.VMEM((POOL, *half), bf16) for _ in range(16)],
            *[pltpu.VMEM((7, 4, 2, *half), bf16) for _ in range(4)],
            *[pltpu.VMEM((4, 2, 4, 2, *half), bf16) for _ in range(4)],
            pltpu.VMEM((14, 1, 128), jnp.int32),
            pltpu.SMEM((14, 1, 128), jnp.int32),
            pltpu.SMEM((SLOTS,), jnp.int32),
            pltpu.VMEM((8, BR), jnp.int32),
            pltpu.VMEM((1, BR), jnp.int32),
            pltpu.VMEM((STEPS, BR), jnp.int32),
            pltpu.VMEM((STEPS * TALL, 2 * HD), bf16),
            pltpu.VMEM((OLD + ROWS, 2 * HD), bf16),
            pltpu.VMEM((OLD + ROWS, 2 * HD), bf16),
            pltpu.VMEM((ROWS, HD), jnp.float32),
            pltpu.VMEM((STEPS * TALL, OLD + ROWS), bf16),
            dma((11,)),
            dma((14,)),
            dma((14,)),
            dma((2, 4, 4)),
            dma((2, 4, 4)),
            dma((4, 2, 3)),
            dma((4, 2, 3)),
            dma((4, 7, 3)),
            dma((4, 4, 2, 3)),
        ],
        compiler_params=pltpu.CompilerParams(
            collective_id=0, has_side_effects=True, vmem_limit_bytes=60 * 1024 * 1024
        ),
        name="rollout_attention",
    )(
        inputs,
        w_qkv.reshape(WIDTH, COLS),
        kv_pool.reshape(POOL, HD, 2 * HD),
        source_block,
        slot_table.T,
        lengths.reshape(1, BR),
        finished,
    )


def solution(mesh):
    placed = (
        P(None, "row", "head"),
        P(None, "head", None),
        P("row", "head", None, None),
        P("row"),
        P("row", None),
        P("row"),
        P(None, "row"),
    )
    return jax.shard_map(
        shards, mesh=mesh, in_specs=placed, out_specs=P(None, "row", "head"), check_vma=False
    )
```

```python
import jax
import jax.numpy as jnp
from jax import lax
from jax.experimental import pallas as pl
from jax.experimental.pallas import tpu as pltpu
from jax.sharding import PartitionSpec as P

HD = 128
GRP = 5
SIDE = 4
RING = 8
STEPS = 4
BR = 64
ROWS = STEPS * BR
SLOTS = 32
POOL = 8
PART = 640
WIDTH = RING * PART
COLS = (GRP + 2) * HD
OLD = SLOTS * HD
HALF = HD // 2
TALL = GRP * BR
NEG = -1.0e30
SCALE = HD ** (-0.5) * 1.4426950408889634
OFFSETS = (0, 1, 3, 2)
MESH = pl.DeviceIdType.MESH
NT = (((1,), (1,)), ((), ()))


def device_row(y, x, core):
    return (y * SIDE + x) * 2 + core


def kernel(
    x_hbm, w_hbm, kv_hbm, sb_hbm, slots_hbm, lens_hbm, fin_hbm, out,
    xb, wb, acc, *rest,
):
    rings = (rest[0:4], rest[4:8], rest[8:12], rest[12:16])
    packs = rest[16:20]
    kept = rest[20:24]
    (
        asks, asked, sb, slots, lens, fin, qa, ka, va, keep, prob, done,
        load_sem, ask_send, ask_recv, z_send, z_recv, r_send, r_recv, p_send, p_recv,
    ) = rest[24:]
    row = lax.axis_index("row")
    head = lax.axis_index("head")
    core = lax.rem(row, 2)
    x = lax.rem(lax.div(row, 2), SIDE)
    y = lax.div(row, 2 * SIDE)

    def around(position, offset, size):
        return lax.rem(position + offset, size)

    above = around(head, 1, RING)
    below = around(head, RING - 1, RING)

    peers = [(device_row(y, x, 1 - core), 1, 1)]
    for step in (1, 2, 3):
        for other in (0, 1):
            back = 4 - step
            peers.append((device_row(around(y, step, SIDE), x, other), 2 + (back - 1) * 2, 2 + (step - 1) * 2 + other))
            peers.append((device_row(y, around(x, step, SIDE), other), 8 + (back - 1) * 2, 8 + (step - 1) * 2 + other))

    barrier = pltpu.get_barrier_semaphore()
    for level in (above, below):
        pl.semaphore_signal(barrier, inc=1, device_id=(row, level), device_id_type=MESH)
    for peer, _, _ in peers:
        pl.semaphore_signal(barrier, inc=1, device_id=(peer, head), device_id_type=MESH)

    started = []

    def send(src, dst, send_sem, recv_sem, to_row, to_head):
        copy = pltpu.make_async_remote_copy(
            src_ref=src, dst_ref=dst, send_sem=send_sem, recv_sem=recv_sem,
            device_id=(to_row, to_head), device_id_type=MESH,
        )
        copy.start()
        started.append(copy)

    def arrived(dst, recv_sem):
        pltpu.make_async_remote_copy(
            src_ref=dst, dst_ref=dst, send_sem=ask_send.at[0], recv_sem=recv_sem,
            device_id=(row, above), device_id_type=MESH,
        ).wait_recv()

    def load(src, dst, index):
        copy = pltpu.make_async_copy(src, dst, load_sem.at[index])
        copy.start()
        return copy

    load_sb = load(sb_hbm, sb, 0)
    load_kv = [
        load(kv_hbm.at[:, pl.ds((kind % 2) * HALF, HALF), pl.ds((kind // 2) * HD, HD)], rings[kind][0], 1 + kind)
        for kind in range(4)
    ]
    load_x = load(x_hbm, xb.at[head], 5)
    load_small = [load(slots_hbm, slots, 6), load(lens_hbm, lens, 7), load(fin_hbm, fin, 8)]
    load_w = load(w_hbm, wb, 9)

    load_sb.wait()
    lane = lax.broadcasted_iota(jnp.int32, (1, 128), 1)
    lowest = jnp.full((1, 128), POOL - 1, jnp.int32)
    highest = jnp.zeros((1, 128), jnp.int32)
    for slot in range(SLOTS):
        block = sb[slot]
        here = lane == jnp.full((1, 128), lax.shift_right_logical(block, 3), jnp.int32)
        inner = jnp.full((1, 128), lax.bitwise_and(block, 7), jnp.int32)
        lowest = jnp.where(here, jnp.minimum(lowest, inner), lowest)
        highest = jnp.where(here, jnp.maximum(highest, inner), highest)
    asks[0] = lowest * 8 + highest
    for copy in load_kv:
        copy.wait()
    load_x.wait()

    pl.semaphore_wait(barrier, len(peers) + 2)

    quarters = (pl.ds(0, 4), pl.ds(4, 4))

    def along(kind, offset):
        if kind % 2 == 0:
            return device_row(y, around(x, offset, SIDE), core)
        return device_row(around(y, offset, SIDE), x, core)

    def ring_start(kind):
        ring = rings[kind]
        for part in (0, 1):
            half = quarters[part]
            send(ring[0].at[half], ring[2].at[half], r_send.at[kind, 0, part], r_recv.at[kind, 0, part], along(kind, 1), head)
            half = quarters[1 - part]
            send(ring[0].at[half], ring[1].at[half], r_send.at[kind, 1, part], r_recv.at[kind, 1, part], along(kind, 3), head)

    def ring_forward(kind):
        ring = rings[kind]
        arrived(ring[2].at[quarters[0]], r_recv.at[kind, 0, 0])
        send(ring[2].at[quarters[0]], ring[3].at[quarters[0]], r_send.at[kind, 0, 2], r_recv.at[kind, 0, 2], along(kind, 1), head)
        arrived(ring[1].at[quarters[1]], r_recv.at[kind, 1, 0])
        send(ring[1].at[quarters[1]], ring[3].at[quarters[1]], r_send.at[kind, 1, 2], r_recv.at[kind, 1, 2], along(kind, 3), head)

    def ring_rest(kind):
        arrived(rings[kind][2].at[quarters[1]], r_recv.at[kind, 0, 1])
        arrived(rings[kind][1].at[quarters[0]], r_recv.at[kind, 1, 1])

    def ring_last(kind):
        arrived(rings[kind][3].at[quarters[0]], r_recv.at[kind, 0, 2])
        arrived(rings[kind][3].at[quarters[1]], r_recv.at[kind, 1, 2])

    level_to = (above, below)

    def z_chunk(way, hop):
        return around(head, RING - hop if way == 0 else hop, RING)

    def z_piece(chunk, way, hop, step):
        if hop == 4:
            return xb.at[chunk, step, pl.ds(way * (BR // 2), BR // 2)]
        return xb.at[chunk, step]

    def z_out(hop, step):
        for way in (0, 1):
            chunk = head if hop == 1 else z_chunk(way, hop - 1)
            ref = z_piece(chunk, way, hop, step)
            send(ref, ref, z_send.at[way, hop - 1, step], z_recv.at[way, hop - 1, step], row, level_to[way])

    def z_in(hop, step, forward=True):
        for way in (0, 1):
            arrived(z_piece(z_chunk(way, hop), way, hop, step), z_recv.at[way, hop - 1, step])
        if forward:
            z_out(hop + 1, step)

    targets = ((2, 0), (2, 1), (1, 0), (3, 0), (1, 1), (3, 1), (0, None))
    batches = ((0, 1), (1, 2), (3, 1))

    def across(kind, offset, to_core):
        if kind % 2 == 0:
            return device_row(around(y, offset, SIDE), x, to_core)
        return device_row(y, around(x, offset, SIDE), to_core)

    def source(kind, turn):
        if kind % 2 == 0:
            return device_row(y, around(x, OFFSETS[turn], SIDE), core)
        return device_row(around(y, OFFSETS[turn], SIDE), x, core)

    def pick(kind, turn, wish, dst):
        chunk = rings[kind][turn]
        code = asked[wish, 0, source(kind, turn)]
        dst[0] = chunk[lax.bitwise_and(lax.shift_right_logical(code, 3), 7)]
        dst[1] = chunk[lax.bitwise_and(code, 7)]

    def cells(seen, from_core, turn, count=1):
        return pl.ds((seen * 2 + from_core) * 8 + turn * 2, count * 2)

    def spread(kind, batch):
        pack, got = packs[kind], kept[kind]
        first, count = batches[batch]
        for turn in range(first, first + count):
            for target, (offset, to_core) in enumerate(targets):
                wish = 1 if target == 6 else (2, 8)[kind % 2] + (offset - 1) * 2 + to_core
                pick(kind, turn, wish, pack.at[target, pl.ds(turn * 2, 2)])
            pick(kind, turn, 0, got.at[cells(0, core, turn)])
        turns = pl.ds(first * 2, count * 2)
        for target, (offset, to_core) in enumerate(targets):
            seen = (4 - offset) % 4
            to_row = device_row(y, x, 1 - core) if target == 6 else across(kind, offset, to_core)
            send(pack.at[target, turns], got.at[cells(seen, core, first, count)], p_send.at[kind, target, batch], p_recv.at[kind, seen, core, batch], to_row, head)

    def collect(kind):
        got = kept[kind]
        for batch in range(3):
            first, count = batches[batch]
            for seen in (1, 3, 2):
                for from_core in (0, 1):
                    arrived(got.at[cells(seen, from_core, first, count)], p_recv.at[kind, seen, from_core, batch])
            arrived(got.at[cells(0, 1 - core, first, count)], p_recv.at[kind, 0, 1 - core, batch])

    def locate():
        spots = []
        for slot in range(SLOTS):
            block = sb[slot]
            device = lax.shift_right_logical(block, 3)
            code = asked[0, 0, device]
            second = jnp.where(lax.bitwise_and(block, 7) == lax.shift_right_logical(code, 3), 0, 1)
            tail = lax.bitwise_and(device, 1) * 8 + second
            off_x = lax.bitwise_and(lax.shift_right_logical(device, 1) + SIDE - x, 3)
            off_y = lax.bitwise_and(lax.shift_right_logical(device, 3) + SIDE - y, 3)
            turn_x = lax.bitwise_xor(off_x, lax.shift_right_logical(off_x, 1))
            turn_y = lax.bitwise_xor(off_y, lax.shift_right_logical(off_y, 1))
            spots.append((off_y * 16 + turn_x * 2 + tail, off_x * 16 + turn_y * 2 + tail))
        return spots

    def fill(table, kinds, spots):
        for slot in range(SLOTS):
            table[pl.ds(slot * HD, HALF), pl.ds(0, HD)] = kept[kinds[0]][spots[slot][0]]
            table[pl.ds(slot * HD + HALF, HALF), pl.ds(0, HD)] = kept[kinds[1]][spots[slot][1]]

    def project(chunk, pair, first=False):
        rows = pl.ds(pair * 2 * BR, 2 * BR)
        part = jnp.dot(
            xb[chunk, pl.ds(pair * 2, 2)].reshape(2 * BR, PART),
            wb[pl.ds(pl.multiple_of(chunk * PART, PART), PART), :],
            preferred_element_type=jnp.float32,
        )
        if first:
            acc[rows, :] = part
        else:
            acc[rows, :] += part

    def round_qkv(pair):
        bf16 = jnp.bfloat16
        for step in (2 * pair, 2 * pair + 1):
            rows = pl.ds(step * BR, BR)
            for group in range(GRP):
                qa[pl.ds(step * TALL + group * BR, BR), pl.ds(0, HD)] = acc[rows, pl.ds(group * HD, HD)].astype(bf16)
            ka[pl.ds(OLD + step * BR, BR), pl.ds(0, HD)] = acc[rows, pl.ds(GRP * HD, HD)].astype(bf16)
            va[pl.ds(OLD + step * BR, BR), pl.ds(0, HD)] = acc[rows, pl.ds((GRP + 1) * HD, HD)].astype(bf16)

    def softmax(step):
        query = qa[pl.ds(step * TALL, TALL), :]
        older = lax.dot_general(query, ka[pl.ds(0, OLD), :], NT, preferred_element_type=jnp.float32)
        newer = lax.dot_general(query, ka[pl.ds(OLD, ROWS), :], NT, preferred_element_type=jnp.float32)
        r = lax.broadcasted_iota(jnp.int32, (TALL, ROWS), 0)
        q = lax.broadcasted_iota(jnp.int32, (TALL, ROWS), 1)
        fresh = jnp.logical_and(lax.bitwise_and(r, BR - 1) == lax.bitwise_and(q, BR - 1), q < (step + 1) * BR)
        newer = jnp.where(fresh, newer, NEG)
        top = jnp.maximum(jnp.max(older, axis=1, keepdims=True), jnp.max(newer, axis=1, keepdims=True))
        prob[pl.ds(step * TALL, TALL), pl.ds(0, OLD)] = jnp.exp2((older - top) * SCALE).astype(jnp.bfloat16)
        prob[pl.ds(step * TALL, TALL), pl.ds(OLD, ROWS)] = jnp.exp2((newer - top) * SCALE).astype(jnp.bfloat16)

    def prepare():
        for copy in load_small:
            copy.wait()
        eye = jnp.where(
            lax.broadcasted_iota(jnp.int32, (BR, BR), 0) == lax.broadcasted_iota(jnp.int32, (BR, BR), 1), 1.0, 0.0
        ).astype(jnp.bfloat16)
        slot_id = lax.broadcasted_iota(jnp.int32, (HD, BR), 0)
        outside = jnp.ones((HD, BR), jnp.float32)
        for entry in range(8):
            named = jnp.where(lens[...] > entry, slots[pl.ds(entry, 1), :], -1)
            outside = jnp.where(slot_id == jnp.broadcast_to(named, (HD, BR)), 0.0, outside)
        outside = lax.dot_general(eye, outside.astype(jnp.bfloat16), NT, preferred_element_type=jnp.float32).astype(jnp.bfloat16)
        for step in range(STEPS):
            going = jnp.where(fin[pl.ds(step, 1), :] > 0, 0.0, 1.0)
            going = jnp.broadcast_to(going, (HD, BR)).astype(jnp.bfloat16)
            keep[pl.ds(step * BR, BR), :] = lax.dot_general(eye, going, NT, preferred_element_type=jnp.float32)
            for group in range(GRP):
                qa[pl.ds(step * TALL + group * BR, BR), pl.ds(HD, HD)] = outside
        column = lax.broadcasted_iota(jnp.int32, (HD, HD), 1)
        for slot in range(SLOTS):
            ka[pl.ds(slot * HD, HD), pl.ds(HD, HD)] = jnp.where(column == slot, NEG, 0.0).astype(jnp.bfloat16)
        ka[pl.ds(OLD, ROWS), :] = jnp.zeros((ROWS, 2 * HD), jnp.bfloat16)
        va[:, pl.ds(HD, HD)] = jnp.ones((OLD + ROWS, HD), jnp.bfloat16)

    for index, (peer, base, mine) in enumerate(peers):
        place = base if base == 1 else base + core
        send(asks.at[0], asks.at[place], ask_send.at[mine], ask_recv.at[place], peer, head)
    ring_start(0)
    ring_start(1)
    z_out(1, 0)
    z_out(1, 1)
    z_out(1, 2)
    ring_start(2)
    ring_start(3)
    prepare()
    ring_forward(0)
    ring_forward(1)
    z_in(1, 0)
    for _, _, mine in peers:
        arrived(asks.at[mine], ask_recv.at[mine])
    to_scalar = pltpu.make_async_copy(asks, asked, load_sem.at[10])
    to_scalar.start()
    to_scalar.wait()
    spread(0, 0)
    spread(1, 0)
    z_in(1, 1)
    z_out(1, 3)
    ring_rest(0)
    ring_rest(1)
    spread(0, 1)
    spread(1, 1)
    z_in(1, 2)
    load_w.wait()
    project(head, 0, True)
    z_in(2, 0)
    ring_last(0)
    ring_last(1)
    spread(0, 2)
    spread(1, 2)
    z_in(2, 1)
    ring_forward(2)
    ring_forward(3)
    z_in(1, 3)
    project(head, 1, True)
    project(z_chunk(0, 1), 0)
    project(z_chunk(1, 1), 0)
    z_in(2, 2)
    spread(2, 0)
    spread(3, 0)
    ring_rest(2)
    ring_rest(3)
    z_in(3, 0)
    spread(2, 1)
    z_in(3, 1)
    spread(3, 1)
    project(z_chunk(0, 2), 0)
    project(z_chunk(1, 2), 0)
    z_in(2, 3)
    project(z_chunk(0, 3), 0)
    project(z_chunk(1, 3), 0)
    z_in(4, 0, False)
    z_in(3, 2)
    z_in(4, 1, False)
    project(z_chunk(0, 4), 0)
    round_qkv(0)
    project(z_chunk(0, 1), 1)
    project(z_chunk(1, 1), 1)
    spots = locate()
    collect(0)
    collect(1)
    fill(ka, (0, 1), spots)
    softmax(0)
    z_in(3, 3)
    ring_last(2)
    ring_last(3)
    spread(2, 2)
    spread(3, 2)
    project(z_chunk(0, 2), 1)
    project(z_chunk(1, 2), 1)
    softmax(1)
    project(z_chunk(0, 3), 1)
    project(z_chunk(1, 3), 1)
    z_in(4, 2, False)
    z_in(4, 3, False)
    project(z_chunk(0, 4), 1)
    round_qkv(1)
    softmax(2)
    softmax(3)
    for copy in started:
        copy.wait_send()
    collect(2)
    collect(3)
    fill(va, (2, 3), spots)
    written = []
    for step in range(STEPS):
        mixed = jnp.dot(prob[pl.ds(step * TALL, TALL), :], va[...], preferred_element_type=jnp.float32)
        going = keep[pl.ds(step * BR, BR), :] > 0.5
        for group in range(GRP):
            part = mixed[group * BR : (group + 1) * BR]
            result = jnp.where(going, part[:, :HD] / part[:, HD:], 0.0).astype(jnp.bfloat16)
            done[step, :, pl.ds(group * HD, HD)] = result
        copy = pltpu.make_async_copy(done.at[step], out.at[step], load_sem.at[11 + step])
        copy.start()
        written.append(copy)
    for copy in written:
        copy.wait()


def shards(inputs, w_qkv, kv_pool, source_block, slot_table, lengths, finished):
    bf16 = jnp.bfloat16
    half = (HALF, HD)
    hbm = pl.BlockSpec(memory_space=pl.ANY)
    dma = pltpu.SemaphoreType.DMA
    return pl.pallas_call(
        kernel,
        out_shape=jax.ShapeDtypeStruct((STEPS, BR, GRP * HD), bf16),
        in_specs=[hbm] * 7,
        out_specs=hbm,
        scratch_shapes=[
            pltpu.VMEM((RING, STEPS, BR, PART), bf16),
            pltpu.VMEM((WIDTH, COLS), bf16),
            pltpu.VMEM((ROWS, COLS), jnp.float32),
            *[pltpu.VMEM((POOL, *half), bf16) for _ in range(16)],
            *[pltpu.VMEM((7, 8, *half), bf16) for _ in range(4)],
            *[pltpu.VMEM((64, *half), bf16) for _ in range(4)],
            pltpu.VMEM((14, 1, 128), jnp.int32),
            pltpu.SMEM((14, 1, 128), jnp.int32),
            pltpu.SMEM((SLOTS,), jnp.int32),
            pltpu.VMEM((8, BR), jnp.int32),
            pltpu.VMEM((1, BR), jnp.int32),
            pltpu.VMEM((STEPS, BR), jnp.int32),
            pltpu.VMEM((STEPS * TALL, 2 * HD), bf16),
            pltpu.VMEM((OLD + ROWS, 2 * HD), bf16),
            pltpu.VMEM((OLD + ROWS, 2 * HD), bf16),
            pltpu.VMEM((ROWS, HD), jnp.float32),
            pltpu.VMEM((STEPS * TALL, OLD + ROWS), bf16),
            pltpu.VMEM((STEPS, BR, GRP * HD), bf16),
            dma((15,)),
            dma((14,)),
            dma((14,)),
            dma((2, 4, 4)),
            dma((2, 4, 4)),
            dma((4, 2, 3)),
            dma((4, 2, 3)),
            dma((4, 7, 3)),
            dma((4, 4, 2, 3)),
        ],
        compiler_params=pltpu.CompilerParams(
            collective_id=0, has_side_effects=True, vmem_limit_bytes=60 * 1024 * 1024
        ),
        name="rollout_attention",
    )(
        inputs,
        w_qkv.reshape(WIDTH, COLS),
        kv_pool.reshape(POOL, HD, 2 * HD),
        source_block,
        slot_table.T,
        lengths.reshape(1, BR),
        finished,
    )


def solution(mesh):
    placed = (
        P(None, "row", "head"),
        P(None, "head", None),
        P("row", "head", None, None),
        P("row"),
        P("row", None),
        P("row"),
        P(None, "row"),
    )
    return jax.shard_map(
        shards, mesh=mesh, in_specs=placed, out_specs=P(None, "row", "head"), check_vma=False
    )
```

```python
import jax
import jax.numpy as jnp
from jax import lax
from jax.experimental import pallas as pl
from jax.experimental.pallas import tpu as pltpu
from jax.sharding import PartitionSpec as P

HD = 128
GRP = 5
SIDE = 4
RING = 8
STEPS = 4
BR = 64
ROWS = STEPS * BR
SLOTS = 32
POOL = 8
PART = 640
WIDTH = RING * PART
COLS = (GRP + 2) * HD
OLD = SLOTS * HD
HALF = HD // 2
QUART = HD // 4
EARLY = SLOTS * HALF
LATE = EARLY + ROWS
TALL = GRP * BR
NEG = -1.0e30
SCALE = HD ** (-0.5) * 1.4426950408889634
OFFSETS = (0, 1, 3, 2)
MESH = pl.DeviceIdType.MESH
NT = (((1,), (1,)), ((), ()))


def device_row(y, x, core):
    return (y * SIDE + x) * 2 + core


def kernel(
    x_hbm, w_hbm, kv_hbm, sb_hbm, slots_hbm, lens_hbm, fin_hbm, out,
    xb, wb, acc, *rest,
):
    rings = (rest[0:4], rest[4:8], rest[8:12], rest[12:16])
    packs = rest[16:22]
    kept = rest[22:28]
    (
        asks, asked, sb, slots, lens, fin, qa, ka, va, keep, prob, half_way, done,
        load_sem, ask_send, ask_recv, z_send, z_recv, r_send, r_recv, p_send, p_recv,
    ) = rest[28:]
    row = lax.axis_index("row")
    head = lax.axis_index("head")
    core = lax.rem(row, 2)
    x = lax.rem(lax.div(row, 2), SIDE)
    y = lax.div(row, 2 * SIDE)

    def around(position, offset, size):
        return lax.rem(position + offset, size)

    above = around(head, 1, RING)
    below = around(head, RING - 1, RING)

    peers = [(device_row(y, x, 1 - core), 1, 1)]
    for step in (1, 2, 3):
        for other in (0, 1):
            back = 4 - step
            peers.append((device_row(around(y, step, SIDE), x, other), 2 + (back - 1) * 2, 2 + (step - 1) * 2 + other))
            peers.append((device_row(y, around(x, step, SIDE), other), 8 + (back - 1) * 2, 8 + (step - 1) * 2 + other))

    barrier = pltpu.get_barrier_semaphore()
    for level in (above, below):
        pl.semaphore_signal(barrier, inc=1, device_id=(row, level), device_id_type=MESH)
    for peer, _, _ in peers:
        pl.semaphore_signal(barrier, inc=1, device_id=(peer, head), device_id_type=MESH)

    started = []

    def send(src, dst, send_sem, recv_sem, to_row, to_head):
        copy = pltpu.make_async_remote_copy(
            src_ref=src, dst_ref=dst, send_sem=send_sem, recv_sem=recv_sem,
            device_id=(to_row, to_head), device_id_type=MESH,
        )
        copy.start()
        started.append(copy)

    def arrived(dst, recv_sem):
        pltpu.make_async_remote_copy(
            src_ref=dst, dst_ref=dst, send_sem=ask_send.at[0], recv_sem=recv_sem,
            device_id=(row, above), device_id_type=MESH,
        ).wait_recv()

    def load(src, dst, index):
        copy = pltpu.make_async_copy(src, dst, load_sem.at[index])
        copy.start()
        return copy

    load_sb = load(sb_hbm, sb, 0)
    load_kv = [
        load(kv_hbm.at[:, pl.ds((kind % 2) * HALF, HALF), pl.ds((kind // 2) * HD, HD)], rings[kind][0], 1 + kind)
        for kind in range(4)
    ]
    load_x = load(x_hbm, xb.at[head], 5)
    load_small = [load(slots_hbm, slots, 6), load(lens_hbm, lens, 7), load(fin_hbm, fin, 8)]
    load_w = load(w_hbm, wb, 9)

    load_sb.wait()
    lane = lax.broadcasted_iota(jnp.int32, (1, 128), 1)
    lowest = jnp.full((1, 128), POOL - 1, jnp.int32)
    highest = jnp.zeros((1, 128), jnp.int32)
    for slot in range(SLOTS):
        block = sb[slot]
        here = lane == jnp.full((1, 128), lax.shift_right_logical(block, 3), jnp.int32)
        inner = jnp.full((1, 128), lax.bitwise_and(block, 7), jnp.int32)
        lowest = jnp.where(here, jnp.minimum(lowest, inner), lowest)
        highest = jnp.where(here, jnp.maximum(highest, inner), highest)
    asks[0] = lowest * 8 + highest
    for copy in load_kv:
        copy.wait()
    load_x.wait()

    pl.semaphore_wait(barrier, len(peers) + 2)

    quarters = (pl.ds(0, 4), pl.ds(4, 4))

    def along(kind, offset):
        if kind % 2 == 0:
            return device_row(y, around(x, offset, SIDE), core)
        return device_row(around(y, offset, SIDE), x, core)

    def ring_start(kind):
        ring = rings[kind]
        for part in (0, 1):
            half = quarters[part]
            send(ring[0].at[half], ring[2].at[half], r_send.at[kind, 0, part], r_recv.at[kind, 0, part], along(kind, 1), head)
            half = quarters[1 - part]
            send(ring[0].at[half], ring[1].at[half], r_send.at[kind, 1, part], r_recv.at[kind, 1, part], along(kind, 3), head)

    def ring_forward(kind):
        ring = rings[kind]
        arrived(ring[2].at[quarters[0]], r_recv.at[kind, 0, 0])
        send(ring[2].at[quarters[0]], ring[3].at[quarters[0]], r_send.at[kind, 0, 2], r_recv.at[kind, 0, 2], along(kind, 1), head)
        arrived(ring[1].at[quarters[1]], r_recv.at[kind, 1, 0])
        send(ring[1].at[quarters[1]], ring[3].at[quarters[1]], r_send.at[kind, 1, 2], r_recv.at[kind, 1, 2], along(kind, 3), head)

    def ring_rest(kind):
        arrived(rings[kind][2].at[quarters[1]], r_recv.at[kind, 0, 1])
        arrived(rings[kind][1].at[quarters[0]], r_recv.at[kind, 1, 1])

    def ring_last(kind):
        arrived(rings[kind][3].at[quarters[0]], r_recv.at[kind, 0, 2])
        arrived(rings[kind][3].at[quarters[1]], r_recv.at[kind, 1, 2])

    level_to = (above, below)

    def z_chunk(way, hop):
        return around(head, RING - hop if way == 0 else hop, RING)

    def z_piece(chunk, way, hop, step):
        if hop == 4:
            return xb.at[chunk, step, pl.ds(way * (BR // 2), BR // 2)]
        return xb.at[chunk, step]

    def z_out(hop, step):
        for way in (0, 1):
            chunk = head if hop == 1 else z_chunk(way, hop - 1)
            ref = z_piece(chunk, way, hop, step)
            send(ref, ref, z_send.at[way, hop - 1, step], z_recv.at[way, hop - 1, step], row, level_to[way])

    def z_in(hop, step, forward=True):
        for way in (0, 1):
            arrived(z_piece(z_chunk(way, hop), way, hop, step), z_recv.at[way, hop - 1, step])
        if forward:
            z_out(hop + 1, step)

    targets = ((2, 0), (2, 1), (1, 0), (3, 0), (1, 1), (3, 1), (0, None))
    batches = (((0, 1), (1, 2), (3, 1)), ((0, 3), (3, 1)), ((0, 4),))

    def across(kind, offset, to_core):
        if kind % 2 == 0:
            return device_row(around(y, offset, SIDE), x, to_core)
        return device_row(y, around(x, offset, SIDE), to_core)

    def source(kind, turn):
        if kind % 2 == 0:
            return device_row(y, around(x, OFFSETS[turn], SIDE), core)
        return device_row(around(y, OFFSETS[turn], SIDE), x, core)

    def pick(stream, turn, wish, dst):
        kind = stream if stream < 4 else stream - 2
        chunk = rings[kind][turn]
        code = asked[wish, 0, source(kind, turn)]
        low = lax.bitwise_and(lax.shift_right_logical(code, 3), 7)
        high = lax.bitwise_and(code, 7)
        if stream < 2:
            dst[0] = chunk[low]
            dst[1] = chunk[high]
        else:
            tokens = pl.ds((stream // 2 - 1) * QUART, QUART)
            dst[0] = chunk[low, tokens]
            dst[1] = chunk[high, tokens]

    def cells(seen, from_core, turn, count=1):
        return pl.ds((seen * 2 + from_core) * 8 + turn * 2, count * 2)

    def spread(stream, batch):
        pack, got = packs[stream], kept[stream]
        first, count = batches[stream // 2][batch]
        for turn in range(first, first + count):
            for target, (offset, to_core) in enumerate(targets):
                wish = 1 if target == 6 else (2, 8)[stream % 2] + (offset - 1) * 2 + to_core
                pick(stream, turn, wish, pack.at[target, pl.ds(turn * 2, 2)])
            pick(stream, turn, 0, got.at[cells(0, core, turn)])
        turns = pl.ds(first * 2, count * 2)
        for target, (offset, to_core) in enumerate(targets):
            seen = (4 - offset) % 4
            to_row = device_row(y, x, 1 - core) if target == 6 else across(stream, offset, to_core)
            send(pack.at[target, turns], got.at[cells(seen, core, first, count)], p_send.at[stream, target, batch], p_recv.at[stream, seen, core, batch], to_row, head)

    def collect(stream):
        got = kept[stream]
        for batch, (first, count) in enumerate(batches[stream // 2]):
            for seen in (1, 3, 2):
                for from_core in (0, 1):
                    arrived(got.at[cells(seen, from_core, first, count)], p_recv.at[stream, seen, from_core, batch])
            arrived(got.at[cells(0, 1 - core, first, count)], p_recv.at[stream, 0, 1 - core, batch])

    def locate():
        spots = []
        for slot in range(SLOTS):
            block = sb[slot]
            device = lax.shift_right_logical(block, 3)
            code = asked[0, 0, device]
            second = jnp.where(lax.bitwise_and(block, 7) == lax.shift_right_logical(code, 3), 0, 1)
            tail = lax.bitwise_and(device, 1) * 8 + second
            off_x = lax.bitwise_and(lax.shift_right_logical(device, 1) + SIDE - x, 3)
            off_y = lax.bitwise_and(lax.shift_right_logical(device, 3) + SIDE - y, 3)
            turn_x = lax.bitwise_xor(off_x, lax.shift_right_logical(off_x, 1))
            turn_y = lax.bitwise_xor(off_y, lax.shift_right_logical(off_y, 1))
            spots.append((off_y * 16 + turn_x * 2 + tail, off_x * 16 + turn_y * 2 + tail))
        return spots

    def fill_keys(spots):
        for slot in range(SLOTS):
            for half in (0, 1):
                block = kept[half][spots[slot][half]]
                ka[pl.ds(slot * HALF + half * QUART, QUART), pl.ds(0, HD)] = block[:QUART]
                ka[pl.ds(LATE + slot * HALF + half * QUART, QUART), pl.ds(0, HD)] = block[QUART:]

    def fill_values(part, spots):
        base = LATE if part else 0
        for slot in range(SLOTS):
            for half in (0, 1):
                va[pl.ds(base + slot * HALF + half * QUART, QUART), pl.ds(0, HD)] = kept[2 + 2 * part + half][spots[slot][half]]

    def project(chunk, pair, first=False):
        rows = pl.ds(pair * 2 * BR, 2 * BR)
        part = jnp.dot(
            xb[chunk, pl.ds(pair * 2, 2)].reshape(2 * BR, PART),
            wb[pl.ds(pl.multiple_of(chunk * PART, PART), PART), :],
            preferred_element_type=jnp.float32,
        )
        if first:
            acc[rows, :] = part
        else:
            acc[rows, :] += part

    def round_qkv(pair):
        bf16 = jnp.bfloat16
        for step in (2 * pair, 2 * pair + 1):
            rows = pl.ds(step * BR, BR)
            for group in range(GRP):
                qa[pl.ds(step * TALL + group * BR, BR), pl.ds(0, HD)] = acc[rows, pl.ds(group * HD, HD)].astype(bf16)
            ka[pl.ds(EARLY + step * BR, BR), pl.ds(0, HD)] = acc[rows, pl.ds(GRP * HD, HD)].astype(bf16)
            va[pl.ds(EARLY + step * BR, BR), pl.ds(0, HD)] = acc[rows, pl.ds((GRP + 1) * HD, HD)].astype(bf16)

    def softmax(step):
        query = qa[pl.ds(step * TALL, TALL), :]
        spans = (pl.ds(0, EARLY), pl.ds(EARLY, ROWS), pl.ds(LATE, EARLY))
        early, newer, late = (
            lax.dot_general(query, ka[span, :], NT, preferred_element_type=jnp.float32) for span in spans
        )
        r = lax.broadcasted_iota(jnp.int32, (TALL, ROWS), 0)
        q = lax.broadcasted_iota(jnp.int32, (TALL, ROWS), 1)
        fresh = jnp.logical_and(lax.bitwise_and(r, BR - 1) == lax.bitwise_and(q, BR - 1), q < (step + 1) * BR)
        newer = jnp.where(fresh, newer, NEG)
        top = jnp.max(newer, axis=1, keepdims=True)
        top = jnp.maximum(top, jnp.maximum(jnp.max(early, axis=1, keepdims=True), jnp.max(late, axis=1, keepdims=True)))
        for span, scores in zip(spans, (early, newer, late)):
            prob[pl.ds(step * TALL, TALL), span] = jnp.exp2((scores - top) * SCALE).astype(jnp.bfloat16)

    def prepare():
        for copy in load_small:
            copy.wait()
        eye = jnp.where(
            lax.broadcasted_iota(jnp.int32, (BR, BR), 0) == lax.broadcasted_iota(jnp.int32, (BR, BR), 1), 1.0, 0.0
        ).astype(jnp.bfloat16)
        slot_id = lax.broadcasted_iota(jnp.int32, (HD, BR), 0)
        outside = jnp.ones((HD, BR), jnp.float32)
        for entry in range(8):
            named = jnp.where(lens[...] > entry, slots[pl.ds(entry, 1), :], -1)
            outside = jnp.where(slot_id == jnp.broadcast_to(named, (HD, BR)), 0.0, outside)
        outside = lax.dot_general(eye, outside.astype(jnp.bfloat16), NT, preferred_element_type=jnp.float32).astype(jnp.bfloat16)
        for step in range(STEPS):
            going = jnp.where(fin[pl.ds(step, 1), :] > 0, 0.0, 1.0)
            going = jnp.broadcast_to(going, (HD, BR)).astype(jnp.bfloat16)
            keep[pl.ds(step * BR, BR), :] = lax.dot_general(eye, going, NT, preferred_element_type=jnp.float32)
            for group in range(GRP):
                qa[pl.ds(step * TALL + group * BR, BR), pl.ds(HD, HD)] = outside
        column = lax.broadcasted_iota(jnp.int32, (HALF, HD), 1)
        for slot in range(SLOTS):
            own = jnp.where(column == slot, NEG, 0.0).astype(jnp.bfloat16)
            ka[pl.ds(slot * HALF, HALF), pl.ds(HD, HD)] = own
            ka[pl.ds(LATE + slot * HALF, HALF), pl.ds(HD, HD)] = own
        ka[pl.ds(EARLY, ROWS), :] = jnp.zeros((ROWS, 2 * HD), jnp.bfloat16)
        va[:, pl.ds(HD, HD)] = jnp.ones((OLD + ROWS, HD), jnp.bfloat16)

    for index, (peer, base, mine) in enumerate(peers):
        place = base if base == 1 else base + core
        send(asks.at[0], asks.at[place], ask_send.at[mine], ask_recv.at[place], peer, head)
    ring_start(0)
    ring_start(1)
    z_out(1, 0)
    z_out(1, 1)
    z_out(1, 2)
    ring_start(2)
    ring_start(3)
    prepare()
    ring_forward(0)
    ring_forward(1)
    z_in(1, 0)
    for _, _, mine in peers:
        arrived(asks.at[mine], ask_recv.at[mine])
    to_scalar = pltpu.make_async_copy(asks, asked, load_sem.at[10])
    to_scalar.start()
    to_scalar.wait()
    spread(0, 0)
    spread(1, 0)
    z_in(1, 1)
    z_out(1, 3)
    ring_rest(0)
    ring_rest(1)
    spread(0, 1)
    spread(1, 1)
    z_in(1, 2)
    load_w.wait()
    project(head, 0, True)
    z_in(2, 0)
    ring_last(0)
    ring_last(1)
    spread(0, 2)
    spread(1, 2)
    z_in(2, 1)
    ring_forward(2)
    ring_forward(3)
    z_in(1, 3)
    project(head, 1, True)
    project(z_chunk(0, 1), 0)
    project(z_chunk(1, 1), 0)
    z_in(2, 2)
    ring_rest(2)
    ring_rest(3)
    spread(2, 0)
    z_in(3, 0)
    spread(3, 0)
    z_in(3, 1)
    project(z_chunk(0, 2), 0)
    project(z_chunk(1, 2), 0)
    z_in(2, 3)
    project(z_chunk(0, 3), 0)
    project(z_chunk(1, 3), 0)
    z_in(4, 0, False)
    z_in(3, 2)
    z_in(4, 1, False)
    project(z_chunk(0, 4), 0)
    round_qkv(0)
    project(z_chunk(0, 1), 1)
    project(z_chunk(1, 1), 1)
    spots = locate()
    collect(0)
    collect(1)
    fill_keys(spots)
    softmax(0)
    ring_last(2)
    ring_last(3)
    spread(2, 1)
    spread(3, 1)
    spread(4, 0)
    spread(5, 0)
    z_in(3, 3)
    project(z_chunk(0, 2), 1)
    project(z_chunk(1, 2), 1)
    softmax(1)
    project(z_chunk(0, 3), 1)
    project(z_chunk(1, 3), 1)
    z_in(4, 2, False)
    z_in(4, 3, False)
    project(z_chunk(0, 4), 1)
    round_qkv(1)
    softmax(2)
    softmax(3)
    collect(2)
    collect(3)
    fill_values(0, spots)
    for step in range(STEPS):
        rows = pl.ds(step * TALL, TALL)
        half_way[rows, :] = jnp.dot(prob[rows, pl.ds(0, LATE)], va[pl.ds(0, LATE), :], preferred_element_type=jnp.float32)
    for copy in started:
        copy.wait_send()
    collect(4)
    collect(5)
    fill_values(1, spots)
    written = []
    for step in range(STEPS):
        rows = pl.ds(step * TALL, TALL)
        mixed = half_way[rows, :] + jnp.dot(prob[rows, pl.ds(LATE, EARLY)], va[pl.ds(LATE, EARLY), :], preferred_element_type=jnp.float32)
        going = keep[pl.ds(step * BR, BR), :] > 0.5
        for group in range(GRP):
            part = mixed[group * BR : (group + 1) * BR]
            result = jnp.where(going, part[:, :HD] / part[:, HD:], 0.0).astype(jnp.bfloat16)
            done[step, :, pl.ds(group * HD, HD)] = result
        copy = pltpu.make_async_copy(done.at[step], out.at[step], load_sem.at[11 + step])
        copy.start()
        written.append(copy)
    for copy in written:
        copy.wait()


def shards(inputs, w_qkv, kv_pool, source_block, slot_table, lengths, finished):
    bf16 = jnp.bfloat16
    half = (HALF, HD)
    hbm = pl.BlockSpec(memory_space=pl.ANY)
    dma = pltpu.SemaphoreType.DMA
    return pl.pallas_call(
        kernel,
        out_shape=jax.ShapeDtypeStruct((STEPS, BR, GRP * HD), bf16),
        in_specs=[hbm] * 7,
        out_specs=hbm,
        scratch_shapes=[
            pltpu.VMEM((RING, STEPS, BR, PART), bf16),
            pltpu.VMEM((WIDTH, COLS), bf16),
            pltpu.VMEM((ROWS, COLS), jnp.float32),
            *[pltpu.VMEM((POOL, *half), bf16) for _ in range(16)],
            *[pltpu.VMEM((7, 8, *half), bf16) for _ in range(2)],
            *[pltpu.VMEM((7, 8, QUART, HD), bf16) for _ in range(4)],
            *[pltpu.VMEM((64, *half), bf16) for _ in range(2)],
            *[pltpu.VMEM((64, QUART, HD), bf16) for _ in range(4)],
            pltpu.VMEM((14, 1, 128), jnp.int32),
            pltpu.SMEM((14, 1, 128), jnp.int32),
            pltpu.SMEM((SLOTS,), jnp.int32),
            pltpu.VMEM((8, BR), jnp.int32),
            pltpu.VMEM((1, BR), jnp.int32),
            pltpu.VMEM((STEPS, BR), jnp.int32),
            pltpu.VMEM((STEPS * TALL, 2 * HD), bf16),
            pltpu.VMEM((OLD + ROWS, 2 * HD), bf16),
            pltpu.VMEM((OLD + ROWS, 2 * HD), bf16),
            pltpu.VMEM((ROWS, HD), jnp.float32),
            pltpu.VMEM((STEPS * TALL, OLD + ROWS), bf16),
            pltpu.VMEM((STEPS * TALL, 2 * HD), jnp.float32),
            pltpu.VMEM((STEPS, BR, GRP * HD), bf16),
            dma((15,)),
            dma((14,)),
            dma((14,)),
            dma((2, 4, 4)),
            dma((2, 4, 4)),
            dma((4, 2, 3)),
            dma((4, 2, 3)),
            dma((6, 7, 3)),
            dma((6, 4, 2, 3)),
        ],
        compiler_params=pltpu.CompilerParams(
            collective_id=0, has_side_effects=True, vmem_limit_bytes=60 * 1024 * 1024
        ),
        name="rollout_attention",
    )(
        inputs,
        w_qkv.reshape(WIDTH, COLS),
        kv_pool.reshape(POOL, HD, 2 * HD),
        source_block,
        slot_table.T,
        lengths.reshape(1, BR),
        finished,
    )


def solution(mesh):
    placed = (
        P(None, "row", "head"),
        P(None, "head", None),
        P("row", "head", None, None),
        P("row"),
        P("row", None),
        P("row"),
        P(None, "row"),
    )
    return jax.shard_map(
        shards, mesh=mesh, in_specs=placed, out_specs=P(None, "row", "head"), check_vma=False
    )
```

```python
import jax
import jax.numpy as jnp
from jax import lax
from jax.experimental import pallas as pl
from jax.experimental.pallas import tpu as pltpu
from jax.sharding import PartitionSpec as P

HD = 128
GRP = 5
SIDE = 4
RING = 8
STEPS = 4
BR = 64
ROWS = STEPS * BR
SLOTS = 32
POOL = 8
PART = 640
WIDTH = RING * PART
COLS = (GRP + 2) * HD
OLD = SLOTS * HD
HALF = HD // 2
QUART = HD // 4
EARLY = SLOTS * HALF
LATE = EARLY + ROWS
TALL = GRP * BR
NEG = -1.0e30
SCALE = HD ** (-0.5) * 1.4426950408889634
OFFSETS = (0, 1, 3, 2)
MESH = pl.DeviceIdType.MESH
NT = (((1,), (1,)), ((), ()))


def device_row(y, x, core):
    return (y * SIDE + x) * 2 + core


def kernel(
    x_hbm, w_hbm, kv_hbm, sb_hbm, slots_hbm, lens_hbm, fin_hbm, out,
    xb, wb, acc, *rest,
):
    rings = (rest[0:4], rest[4:8], rest[8:12], rest[12:16])
    packs = rest[16:20]
    kept = rest[20:26]
    (
        asks, asked, sb, slots, lens, fin, qa, ka, va, keep, prob, half_way, done,
        load_sem, ask_send, ask_recv, z_send, z_recv, r_send, r_recv, p_send, p_recv,
    ) = rest[26:]
    row = lax.axis_index("row")
    head = lax.axis_index("head")
    core = lax.rem(row, 2)
    x = lax.rem(lax.div(row, 2), SIDE)
    y = lax.div(row, 2 * SIDE)

    def around(position, offset, size):
        return lax.rem(position + offset, size)

    above = around(head, 1, RING)
    below = around(head, RING - 1, RING)

    peers = [(device_row(y, x, 1 - core), 1, 1)]
    for step in (1, 2, 3):
        for other in (0, 1):
            back = 4 - step
            peers.append((device_row(around(y, step, SIDE), x, other), 2 + (back - 1) * 2, 2 + (step - 1) * 2 + other))
            peers.append((device_row(y, around(x, step, SIDE), other), 8 + (back - 1) * 2, 8 + (step - 1) * 2 + other))

    barrier = pltpu.get_barrier_semaphore()
    for level in (above, below):
        pl.semaphore_signal(barrier, inc=1, device_id=(row, level), device_id_type=MESH)
    for peer, _, _ in peers:
        pl.semaphore_signal(barrier, inc=1, device_id=(peer, head), device_id_type=MESH)

    started = []

    def send(src, dst, send_sem, recv_sem, to_row, to_head):
        copy = pltpu.make_async_remote_copy(
            src_ref=src, dst_ref=dst, send_sem=send_sem, recv_sem=recv_sem,
            device_id=(to_row, to_head), device_id_type=MESH,
        )
        copy.start()
        started.append(copy)

    def arrived(dst, recv_sem):
        pltpu.make_async_remote_copy(
            src_ref=dst, dst_ref=dst, send_sem=ask_send.at[0], recv_sem=recv_sem,
            device_id=(row, above), device_id_type=MESH,
        ).wait_recv()

    def load(src, dst, index):
        copy = pltpu.make_async_copy(src, dst, load_sem.at[index])
        copy.start()
        return copy

    load_sb = load(sb_hbm, sb, 0)
    load_kv = [
        load(kv_hbm.at[:, pl.ds((kind % 2) * HALF, HALF), pl.ds((kind // 2) * HD, HD)], rings[kind][0], 1 + kind)
        for kind in range(4)
    ]
    load_x = load(x_hbm, xb.at[head], 5)
    load_small = [load(slots_hbm, slots, 6), load(lens_hbm, lens, 7), load(fin_hbm, fin, 8)]
    load_w = load(w_hbm, wb, 9)

    load_sb.wait()
    lane = lax.broadcasted_iota(jnp.int32, (1, 128), 1)
    lowest = jnp.full((1, 128), POOL - 1, jnp.int32)
    highest = jnp.zeros((1, 128), jnp.int32)
    for slot in range(SLOTS):
        block = sb[slot]
        here = lane == jnp.full((1, 128), lax.shift_right_logical(block, 3), jnp.int32)
        inner = jnp.full((1, 128), lax.bitwise_and(block, 7), jnp.int32)
        lowest = jnp.where(here, jnp.minimum(lowest, inner), lowest)
        highest = jnp.where(here, jnp.maximum(highest, inner), highest)
    asks[0] = lowest * 8 + highest
    for copy in load_kv:
        copy.wait()
    load_x.wait()

    pl.semaphore_wait(barrier, len(peers) + 2)

    quarters = (pl.ds(0, 4), pl.ds(4, 4))

    def along(kind, offset):
        if kind % 2 == 0:
            return device_row(y, around(x, offset, SIDE), core)
        return device_row(around(y, offset, SIDE), x, core)

    def ring_start(kind):
        ring = rings[kind]
        for part in (0, 1):
            half = quarters[part]
            send(ring[0].at[half], ring[2].at[half], r_send.at[kind, 0, part], r_recv.at[kind, 0, part], along(kind, 1), head)
            half = quarters[1 - part]
            send(ring[0].at[half], ring[1].at[half], r_send.at[kind, 1, part], r_recv.at[kind, 1, part], along(kind, 3), head)

    def ring_forward(kind):
        ring = rings[kind]
        arrived(ring[2].at[quarters[0]], r_recv.at[kind, 0, 0])
        send(ring[2].at[quarters[0]], ring[3].at[quarters[0]], r_send.at[kind, 0, 2], r_recv.at[kind, 0, 2], along(kind, 1), head)
        arrived(ring[1].at[quarters[1]], r_recv.at[kind, 1, 0])
        send(ring[1].at[quarters[1]], ring[3].at[quarters[1]], r_send.at[kind, 1, 2], r_recv.at[kind, 1, 2], along(kind, 3), head)

    def ring_rest(kind):
        arrived(rings[kind][2].at[quarters[1]], r_recv.at[kind, 0, 1])
        arrived(rings[kind][1].at[quarters[0]], r_recv.at[kind, 1, 1])

    def ring_last(kind):
        arrived(rings[kind][3].at[quarters[0]], r_recv.at[kind, 0, 2])
        arrived(rings[kind][3].at[quarters[1]], r_recv.at[kind, 1, 2])

    level_to = (above, below)

    def z_chunk(way, hop):
        return around(head, RING - hop if way == 0 else hop, RING)

    def z_piece(chunk, way, hop, step):
        if hop == 4:
            return xb.at[chunk, step, pl.ds(way * (BR // 2), BR // 2)]
        return xb.at[chunk, step]

    def z_out(hop, step):
        for way in (0, 1):
            chunk = head if hop == 1 else z_chunk(way, hop - 1)
            ref = z_piece(chunk, way, hop, step)
            send(ref, ref, z_send.at[way, hop - 1, step], z_recv.at[way, hop - 1, step], row, level_to[way])

    def z_in(hop, step, forward=True):
        for way in (0, 1):
            arrived(z_piece(z_chunk(way, hop), way, hop, step), z_recv.at[way, hop - 1, step])
        if forward:
            z_out(hop + 1, step)

    targets = ((2, 0), (2, 1), (1, 0), (3, 0), (1, 1), (3, 1), (0, None))
    batches = (((0, 1), (1, 2), (3, 1)), ((0, 3), (3, 1)), ((0, 4),))

    def across(kind, offset, to_core):
        if kind % 2 == 0:
            return device_row(around(y, offset, SIDE), x, to_core)
        return device_row(y, around(x, offset, SIDE), to_core)

    def source(kind, turn):
        if kind % 2 == 0:
            return device_row(y, around(x, OFFSETS[turn], SIDE), core)
        return device_row(around(y, OFFSETS[turn], SIDE), x, core)

    def pick(kind, turn, wish):
        code = asked[wish, 0, source(kind, turn)]
        chunk = rings[kind][turn]
        return chunk[lax.bitwise_and(lax.shift_right_logical(code, 3), 7)], chunk[lax.bitwise_and(code, 7)]

    def cells(seen, from_core, turn, count=1):
        return pl.ds((seen * 2 + from_core) * 8 + turn * 2, count * 2)

    def pack_turn(kind, turn):
        for target, (offset, to_core) in enumerate(targets):
            wish = 1 if target == 6 else (2, 8)[kind % 2] + (offset - 1) * 2 + to_core
            packs[kind][target, pl.ds(turn * 2, 2)] = jnp.stack(pick(kind, turn, wish))
        for which, block in enumerate(pick(kind, turn, 0)):
            at = (core * 8) + turn * 2 + which
            if kind < 2:
                kept[kind][at] = block
            else:
                kept[kind][at] = block[:QUART]
                kept[kind + 2][at] = block[QUART:]

    def spread(stream, batch, packed=False):
        kind = stream if stream < 4 else stream - 2
        pack, got = packs[kind], kept[stream]
        first, count = batches[stream // 2][batch]
        if not packed:
            for turn in range(first, first + count):
                pack_turn(kind, turn)
        turns = pl.ds(first * 2, count * 2)
        for target, (offset, to_core) in enumerate(targets):
            seen = (4 - offset) % 4
            to_row = device_row(y, x, 1 - core) if target == 6 else across(stream, offset, to_core)
            src = pack.at[target, turns]
            if stream >= 2:
                src = pack.at[target, turns, pl.ds((stream // 2 - 1) * QUART, QUART)]
            send(src, got.at[cells(seen, core, first, count)], p_send.at[stream, target, batch], p_recv.at[stream, seen, core, batch], to_row, head)

    def collect(stream):
        got = kept[stream]
        for batch, (first, count) in enumerate(batches[stream // 2]):
            for seen in (1, 3, 2):
                for from_core in (0, 1):
                    arrived(got.at[cells(seen, from_core, first, count)], p_recv.at[stream, seen, from_core, batch])
            arrived(got.at[cells(0, 1 - core, first, count)], p_recv.at[stream, 0, 1 - core, batch])

    def locate():
        spots = []
        for slot in range(SLOTS):
            block = sb[slot]
            device = lax.shift_right_logical(block, 3)
            code = asked[0, 0, device]
            second = jnp.where(lax.bitwise_and(block, 7) == lax.shift_right_logical(code, 3), 0, 1)
            tail = lax.bitwise_and(device, 1) * 8 + second
            off_x = lax.bitwise_and(lax.shift_right_logical(device, 1) + SIDE - x, 3)
            off_y = lax.bitwise_and(lax.shift_right_logical(device, 3) + SIDE - y, 3)
            turn_x = lax.bitwise_xor(off_x, lax.shift_right_logical(off_x, 1))
            turn_y = lax.bitwise_xor(off_y, lax.shift_right_logical(off_y, 1))
            spots.append((off_y * 16 + turn_x * 2 + tail, off_x * 16 + turn_y * 2 + tail))
        return spots

    def fill_keys(spots):
        for slot in range(SLOTS):
            for half in (0, 1):
                block = kept[half][spots[slot][half]]
                ka[pl.ds(slot * HALF + half * QUART, QUART), pl.ds(0, HD)] = block[:QUART]
                ka[pl.ds(LATE + slot * HALF + half * QUART, QUART), pl.ds(0, HD)] = block[QUART:]

    def fill_values(part, spots):
        base = LATE if part else 0
        for slot in range(SLOTS):
            for half in (0, 1):
                va[pl.ds(base + slot * HALF + half * QUART, QUART), pl.ds(0, HD)] = kept[2 + 2 * part + half][spots[slot][half]]

    def project(chunk, pair, first=False):
        rows = pl.ds(pair * 2 * BR, 2 * BR)
        part = jnp.dot(
            xb[chunk, pl.ds(pair * 2, 2)].reshape(2 * BR, PART),
            wb[pl.ds(pl.multiple_of(chunk * PART, PART), PART), :],
            preferred_element_type=jnp.float32,
        )
        if first:
            acc[rows, :] = part
        else:
            acc[rows, :] += part

    def round_qkv(pair):
        bf16 = jnp.bfloat16
        for step in (2 * pair, 2 * pair + 1):
            rows = pl.ds(step * BR, BR)
            for group in range(GRP):
                qa[pl.ds(step * TALL + group * BR, BR), pl.ds(0, HD)] = acc[rows, pl.ds(group * HD, HD)].astype(bf16)
            ka[pl.ds(EARLY + step * BR, BR), pl.ds(0, HD)] = acc[rows, pl.ds(GRP * HD, HD)].astype(bf16)
            va[pl.ds(EARLY + step * BR, BR), pl.ds(0, HD)] = acc[rows, pl.ds((GRP + 1) * HD, HD)].astype(bf16)

    def softmax(step):
        query = qa[pl.ds(step * TALL, TALL), :]
        spans = (pl.ds(0, EARLY), pl.ds(EARLY, ROWS), pl.ds(LATE, EARLY))
        early, newer, late = (
            lax.dot_general(query, ka[span, :], NT, preferred_element_type=jnp.float32) for span in spans
        )
        r = lax.broadcasted_iota(jnp.int32, (TALL, ROWS), 0)
        q = lax.broadcasted_iota(jnp.int32, (TALL, ROWS), 1)
        fresh = jnp.logical_and(lax.bitwise_and(r, BR - 1) == lax.bitwise_and(q, BR - 1), q < (step + 1) * BR)
        newer = jnp.where(fresh, newer, NEG)
        top = jnp.max(newer, axis=1, keepdims=True)
        top = jnp.maximum(top, jnp.maximum(jnp.max(early, axis=1, keepdims=True), jnp.max(late, axis=1, keepdims=True)))
        for span, scores in zip(spans, (early, newer, late)):
            prob[pl.ds(step * TALL, TALL), span] = jnp.exp2((scores - top) * SCALE).astype(jnp.bfloat16)

    def prepare():
        for copy in load_small:
            copy.wait()
        eye = jnp.where(
            lax.broadcasted_iota(jnp.int32, (BR, BR), 0) == lax.broadcasted_iota(jnp.int32, (BR, BR), 1), 1.0, 0.0
        ).astype(jnp.bfloat16)
        slot_id = lax.broadcasted_iota(jnp.int32, (HD, BR), 0)
        outside = jnp.ones((HD, BR), jnp.float32)
        for entry in range(8):
            named = jnp.where(lens[...] > entry, slots[pl.ds(entry, 1), :], -1)
            outside = jnp.where(slot_id == jnp.broadcast_to(named, (HD, BR)), 0.0, outside)
        outside = lax.dot_general(eye, outside.astype(jnp.bfloat16), NT, preferred_element_type=jnp.float32).astype(jnp.bfloat16)
        for step in range(STEPS):
            going = jnp.where(fin[pl.ds(step, 1), :] > 0, 0.0, 1.0)
            going = jnp.broadcast_to(going, (HD, BR)).astype(jnp.bfloat16)
            keep[pl.ds(step * BR, BR), :] = lax.dot_general(eye, going, NT, preferred_element_type=jnp.float32)
            for group in range(GRP):
                qa[pl.ds(step * TALL + group * BR, BR), pl.ds(HD, HD)] = outside
        column = lax.broadcasted_iota(jnp.int32, (HALF, HD), 1)
        for slot in range(SLOTS):
            own = jnp.where(column == slot, NEG, 0.0).astype(jnp.bfloat16)
            ka[pl.ds(slot * HALF, HALF), pl.ds(HD, HD)] = own
            ka[pl.ds(LATE + slot * HALF, HALF), pl.ds(HD, HD)] = own
        ka[pl.ds(EARLY, ROWS), :] = jnp.zeros((ROWS, 2 * HD), jnp.bfloat16)
        va[:, pl.ds(HD, HD)] = jnp.ones((OLD + ROWS, HD), jnp.bfloat16)

    for index, (peer, base, mine) in enumerate(peers):
        place = base if base == 1 else base + core
        send(asks.at[0], asks.at[place], ask_send.at[mine], ask_recv.at[place], peer, head)
    ring_start(0)
    ring_start(1)
    z_out(1, 0)
    z_out(1, 1)
    z_out(1, 2)
    ring_start(2)
    ring_start(3)
    prepare()
    ring_forward(0)
    ring_forward(1)
    z_in(1, 0)
    for _, _, mine in peers:
        arrived(asks.at[mine], ask_recv.at[mine])
    to_scalar = pltpu.make_async_copy(asks, asked, load_sem.at[10])
    to_scalar.start()
    to_scalar.wait()
    spread(0, 0)
    spread(1, 0)
    z_in(1, 1)
    z_out(1, 3)
    ring_rest(0)
    ring_rest(1)
    spread(0, 1)
    spread(1, 1)
    z_in(1, 2)
    load_w.wait()
    project(head, 0, True)
    z_in(2, 0)
    ring_last(0)
    ring_last(1)
    spread(0, 2)
    spread(1, 2)
    z_in(2, 1)
    ring_forward(2)
    ring_forward(3)
    z_in(1, 3)
    project(head, 1, True)
    project(z_chunk(0, 1), 0)
    project(z_chunk(1, 1), 0)
    z_in(2, 2)
    ring_rest(2)
    ring_rest(3)
    pack_turn(2, 0)
    pack_turn(3, 0)
    z_in(3, 0)
    pack_turn(2, 1)
    pack_turn(3, 1)
    z_in(3, 1)
    pack_turn(2, 2)
    pack_turn(3, 2)
    spread(2, 0, True)
    spread(3, 0, True)
    z_in(2, 3)
    project(z_chunk(0, 2), 0)
    project(z_chunk(1, 2), 0)
    project(z_chunk(0, 3), 0)
    project(z_chunk(1, 3), 0)
    z_in(4, 0, False)
    z_in(3, 2)
    z_in(4, 1, False)
    project(z_chunk(0, 4), 0)
    round_qkv(0)
    project(z_chunk(0, 1), 1)
    project(z_chunk(1, 1), 1)
    spots = locate()
    collect(0)
    collect(1)
    fill_keys(spots)
    softmax(0)
    ring_last(2)
    ring_last(3)
    spread(2, 1)
    spread(3, 1)
    spread(4, 0, True)
    spread(5, 0, True)
    z_in(3, 3)
    project(z_chunk(0, 2), 1)
    project(z_chunk(1, 2), 1)
    softmax(1)
    project(z_chunk(0, 3), 1)
    project(z_chunk(1, 3), 1)
    z_in(4, 2, False)
    z_in(4, 3, False)
    project(z_chunk(0, 4), 1)
    round_qkv(1)
    softmax(2)
    softmax(3)
    collect(2)
    collect(3)
    fill_values(0, spots)
    for step in range(STEPS):
        rows = pl.ds(step * TALL, TALL)
        half_way[rows, :] = jnp.dot(prob[rows, pl.ds(0, LATE)], va[pl.ds(0, LATE), :], preferred_element_type=jnp.float32)
    for copy in started:
        copy.wait_send()
    collect(4)
    collect(5)
    fill_values(1, spots)
    written = []
    for step in range(STEPS):
        rows = pl.ds(step * TALL, TALL)
        mixed = half_way[rows, :] + jnp.dot(prob[rows, pl.ds(LATE, EARLY)], va[pl.ds(LATE, EARLY), :], preferred_element_type=jnp.float32)
        going = keep[pl.ds(step * BR, BR), :] > 0.5
        for group in range(GRP):
            part = mixed[group * BR : (group + 1) * BR]
            result = jnp.where(going, part[:, :HD] / part[:, HD:], 0.0).astype(jnp.bfloat16)
            done[step, :, pl.ds(group * HD, HD)] = result
        copy = pltpu.make_async_copy(done.at[step], out.at[step], load_sem.at[11 + step])
        copy.start()
        written.append(copy)
    for copy in written:
        copy.wait()


def shards(inputs, w_qkv, kv_pool, source_block, slot_table, lengths, finished):
    bf16 = jnp.bfloat16
    half = (HALF, HD)
    hbm = pl.BlockSpec(memory_space=pl.ANY)
    dma = pltpu.SemaphoreType.DMA
    return pl.pallas_call(
        kernel,
        out_shape=jax.ShapeDtypeStruct((STEPS, BR, GRP * HD), bf16),
        in_specs=[hbm] * 7,
        out_specs=hbm,
        scratch_shapes=[
            pltpu.VMEM((RING, STEPS, BR, PART), bf16),
            pltpu.VMEM((WIDTH, COLS), bf16),
            pltpu.VMEM((ROWS, COLS), jnp.float32),
            *[pltpu.VMEM((POOL, *half), bf16) for _ in range(16)],
            *[pltpu.VMEM((7, 8, *half), bf16) for _ in range(4)],
            *[pltpu.VMEM((64, *half), bf16) for _ in range(2)],
            *[pltpu.VMEM((64, QUART, HD), bf16) for _ in range(4)],
            pltpu.VMEM((14, 1, 128), jnp.int32),
            pltpu.SMEM((14, 1, 128), jnp.int32),
            pltpu.SMEM((SLOTS,), jnp.int32),
            pltpu.VMEM((8, BR), jnp.int32),
            pltpu.VMEM((1, BR), jnp.int32),
            pltpu.VMEM((STEPS, BR), jnp.int32),
            pltpu.VMEM((STEPS * TALL, 2 * HD), bf16),
            pltpu.VMEM((OLD + ROWS, 2 * HD), bf16),
            pltpu.VMEM((OLD + ROWS, 2 * HD), bf16),
            pltpu.VMEM((ROWS, HD), jnp.float32),
            pltpu.VMEM((STEPS * TALL, OLD + ROWS), bf16),
            pltpu.VMEM((STEPS * TALL, 2 * HD), jnp.float32),
            pltpu.VMEM((STEPS, BR, GRP * HD), bf16),
            dma((15,)),
            dma((14,)),
            dma((14,)),
            dma((2, 4, 4)),
            dma((2, 4, 4)),
            dma((4, 2, 3)),
            dma((4, 2, 3)),
            dma((6, 7, 3)),
            dma((6, 4, 2, 3)),
        ],
        compiler_params=pltpu.CompilerParams(
            collective_id=0, has_side_effects=True, vmem_limit_bytes=60 * 1024 * 1024
        ),
        name="rollout_attention",
    )(
        inputs,
        w_qkv.reshape(WIDTH, COLS),
        kv_pool.reshape(POOL, HD, 2 * HD),
        source_block,
        slot_table.T,
        lengths.reshape(1, BR),
        finished,
    )


def solution(mesh):
    placed = (
        P(None, "row", "head"),
        P(None, "head", None),
        P("row", "head", None, None),
        P("row"),
        P("row", None),
        P("row"),
        P(None, "row"),
    )
    return jax.shard_map(
        shards, mesh=mesh, in_specs=placed, out_specs=P(None, "row", "head"), check_vma=False
    )
```
